32 devices in a mesh: shot: 2 (over y), slab: 4 (over z), rep: 2 (over x), sub: 2 (over core).
Axes of the slice: x: 2, y: 2, z: 4, core: 2. Of those that a mesh axis runs over, the one named last changes fastest.
Arguments:
- courant: float32 [16, 32, 256], P('slab', 'sub'), may hold values from 0.2 to 0.42
- incident_prev: float32 [32, 32, 256], P(('shot', 'slab'), 'sub', 'rep'), parts along dimension 0, may hold values from -6 to 6
- incident_now: float32 [32, 32, 256], P(('shot', 'slab'), 'sub', 'rep'), parts along dimension 0, may hold values from -6 to 6
- wavelet: float32 [4, 8], replicated, may hold values from -6 to 6
- source_z: int32 [16], P('shot'), parts along dimension 0, may hold values from 0 to 15
- source_y: int32 [16], P('shot'), parts along dimension 0, may hold values from 0 to 31
- source_x: int32 [16], P('shot'), parts along dimension 0, may hold values from 0 to 255
- replica_seeds: int32 [4], P('rep'), may hold values from 0 to 999999
- receiver_z: int32 [32], replicated, may hold values from 0 to 15, as said below
- receiver_y: int32 [32], replicated, may hold values from 0 to 31, as said below
- receiver_x: int32 [32], replicated, may hold values from 0 to 255, as said below
Outputs:
- incident_final: float32 [32, 32, 256], P(('shot', 'slab'), 'sub', 'rep'), parts along dimension 0
- scattered_final: float32 [4, 32, 32, 256], P('rep', ('shot', 'slab'), 'sub'), parts along dimension 1
- traces: float32 [8, 4, 32], P('shot', 'rep'), parts along dimension 0
The draws below stay inside these ranges and needn't reach their ends.
There are 2 independent parts, one for each index of `shot`. The reference program is written for one: setup_inputs(seed, part) draws one part's arguments, and reference() takes and returns one part's arrays. A program takes and returns all parts, laid end to end along the dimension named above; an argument that names none is the same for every part. Nothing has to cross between parts.
Inputs may be any that keep to these rules, and one draw needn't show every extreme that they name: `receiver_z`: receiver j lies at a depth from (j // 8) * 4 to that plus 4 - 1; the first receiver is at depth 0 and the last at depth 16 - 1. `receiver_y`: receiver j lies at a second coordinate from ((j // 4) % 2) * 16 to that plus 16 - 1; the first receiver is at 0 and the last at 31. `receiver_x`: the first receiver is at 0 and the last at 255.
All inputs are finite; a program needn't handle non-finite values.
Results may differ from the reference program's by a relative error of at most 0.00002.
Values sent between devices are 32-bit elements; how exact they have to be, the bound alone decides.
A program may use at most 64 MiB of HBM per device.

```python
import math
import jax
import jax.numpy as jnp
from jax import lax

CZ = 4
CY = 16
NX = 256
STEPS = 4
NSRC = 8
REC_DEV = 4
NZ = 16
NY = 32
REPS = 4
NREC = 32


def draw_receiver_z(key, part):
    index = jnp.arange(NREC, dtype=jnp.int32)
    slab_of = index // (REC_DEV * (NY // CY))
    offsets = jax.random.randint(jax.random.fold_in(key, 11), (NREC,), 0, CZ, dtype=jnp.int32)
    offsets = offsets.at[0].set(0).at[NREC - 1].set(CZ - 1)
    return slab_of * CZ + offsets


def draw_receiver_y(key, part):
    index = jnp.arange(NREC, dtype=jnp.int32)
    block_of = index // REC_DEV % (NY // CY)
    offsets = jax.random.randint(jax.random.fold_in(key, 23), (NREC,), 0, CY, dtype=jnp.int32)
    offsets = offsets.at[0].set(0).at[NREC - 1].set(CY - 1)
    return block_of * CY + offsets


def draw_receiver_x(key, part):
    offsets = jax.random.randint(jax.random.fold_in(key, 37), (NREC,), 0, NX, dtype=jnp.int32)
    return offsets.at[0].set(0).at[NREC - 1].set(NX - 1)


def set_ends(result, own_key, smallest, high):
    shape = result.shape
    place = [jax.random.randint(jax.random.fold_in(own_key, axis), (), 0, shape[axis]) for axis in range(len(shape))]
    result = result.at[tuple(place)].set(smallest)
    longest = shape.index(max(shape))
    place[longest] = (place[longest] + 1) % shape[longest]
    return result.at[tuple(place)].set(high)


def levels(rng, dims, shards, least, largest):
    def one(dim, shards_of):
        heights = jax.random.uniform(jax.random.fold_in(jax.random.fold_in(rng, 6), dim), (shards_of,), jnp.float32, least / len(shards), largest / len(shards))
        return jnp.repeat(jnp.exp(heights), dims[dim] // shards_of).reshape((-1,) + (1,) * (len(dims) - dim - 1))

    loudness = one(*shards[0])
    for cut in shards[1:]:
        loudness = loudness * one(*cut)
    return loudness


def normal_values(stream_key, dims, deviation, most, shards=(), held_as=jnp.bfloat16):
    result = deviation * jax.random.normal(stream_key, dims, jnp.float32)
    if shards:
        result = result * levels(stream_key, dims, shards, -0.22, 0.18)
    return jnp.clip(result, -most, most).astype(held_as)


def setup_inputs(seed: int = 0, part: int = 0) -> dict:
    splits = jax.random.split(jax.random.key(seed), 12)
    own_keys = jax.random.split(jax.random.fold_in(splits[11], part), 12)
    courant = jnp.clip(jnp.exp(math.log(0.42) - 0.7419373 * jax.random.uniform(splits[0], (NZ, NY, NX), jnp.float32) ** levels(splits[0], (NZ, NY, NX), ((0, 4), (1, 2)), -0.2, 0.2)), 0.2, 0.42)
    incident_prev = normal_values(own_keys[1], (NZ, NY, NX), 1.0, 6.0, ((0, 4), (1, 2), (2, 2)), jnp.float32)
    incident_now = normal_values(own_keys[2], (NZ, NY, NX), 1.0, 6.0, ((0, 4), (1, 2), (2, 2)), jnp.float32)
    wavelet = normal_values(splits[3], (STEPS, NSRC), 1.0, 6.0, (), jnp.float32)
    source_z = set_ends(jax.random.randint(own_keys[4], (NSRC,), 0, NZ), jax.random.fold_in(own_keys[4], 1), 0, NZ - 1).astype(jnp.int32)
    source_y = set_ends(jax.random.randint(own_keys[5], (NSRC,), 0, NY), jax.random.fold_in(own_keys[5], 1), 0, NY - 1).astype(jnp.int32)
    source_x = set_ends(jax.random.randint(own_keys[6], (NSRC,), 0, NX), jax.random.fold_in(own_keys[6], 1), 0, NX - 1).astype(jnp.int32)
    replica_seeds = set_ends(jax.random.randint(splits[7], (REPS,), 0, 1000000), jax.random.fold_in(splits[7], 1), 0, 999999).astype(jnp.int32)
    receiver_z = draw_receiver_z(jax.random.fold_in(splits[11], 71), part)
    receiver_y = draw_receiver_y(jax.random.fold_in(splits[11], 71), part)
    receiver_x = draw_receiver_x(jax.random.fold_in(splits[11], 71), part)
    return dict(courant=courant, incident_prev=incident_prev, incident_now=incident_now, wavelet=wavelet, source_z=source_z, source_y=source_y, source_x=source_x, replica_seeds=replica_seeds, receiver_z=receiver_z, receiver_y=receiver_y, receiver_x=receiver_x)


stencil_coeffs = (-205.0 / 72.0, 8.0 / 5.0, -1.0 / 5.0, 8.0 / 315.0, -1.0 / 560.0)
pert_scale = 0.2


def laplace(padded):
    deep_count = padded.shape[-3] - 8
    tall_count = padded.shape[-2] - 8
    wide_count = padded.shape[-1] - 8

    def window(shift_z, shift_y, shift_x):
        return padded[..., 4 + shift_z:4 + shift_z + deep_count, 4 + shift_y:4 + shift_y + tall_count, 4 + shift_x:4 + shift_x + wide_count]

    summed = (3.0 * stencil_coeffs[0]) * window(0, 0, 0)
    for offset in range(1, 5):
        couple = window(offset, 0, 0) + window(-offset, 0, 0) + window(0, offset, 0) + window(0, -offset, 0) + window(0, 0, offset) + window(0, 0, -offset)
        summed = summed + stencil_coeffs[offset] * couple
    return summed


def perturbation(seed_values, depth_coord, height_coord, width_coord):
    hashed = (seed_values[:, None, None, None] * 668265263 + depth_coord[None, :, None, None] * 73856093 + height_coord[None, None, :, None] * 19349663 + width_coord[None, None, None, :] * 83492791)
    hashed = jnp.bitwise_xor(hashed, jnp.right_shift(hashed, 15))
    hashed = hashed * 1274126177
    hashed = jnp.bitwise_xor(hashed, jnp.right_shift(hashed, 13))
    fraction = jnp.bitwise_and(hashed, 65535).astype(jnp.float32) / 65535.0
    return pert_scale * (2.0 * fraction - 1.0)


def inject(field, amounts, where_z, where_y, where_x, start_z, start_y, start_x):
    local_z = where_z - start_z
    local_y = where_y - start_y
    local_x = where_x - start_x
    inside = (local_z >= 0) & (local_z < field.shape[0]) & (local_y >= 0) & (local_y < field.shape[1]) & (local_x >= 0) & (local_x < field.shape[2])
    clip_z = jnp.clip(local_z, 0, field.shape[0] - 1).astype(jnp.int32)
    clip_y = jnp.clip(local_y, 0, field.shape[1] - 1).astype(jnp.int32)
    clip_x = jnp.clip(local_x, 0, field.shape[2] - 1).astype(jnp.int32)
    return field.at[clip_z, clip_y, clip_x].add(jnp.where(inside, amounts, jnp.zeros_like(amounts)))


def sample(field, where_z, where_y, where_x, start_z, start_y):
    local_z = where_z - start_z
    local_y = where_y - start_y
    inside = (local_z >= 0) & (local_z < field.shape[1]) & (local_y >= 0) & (local_y < field.shape[2])
    clip_z = jnp.clip(local_z, 0, field.shape[1] - 1).astype(jnp.int32)
    clip_y = jnp.clip(local_y, 0, field.shape[2] - 1).astype(jnp.int32)
    picked = field[:, clip_z, clip_y, where_x.astype(jnp.int32)]
    return jnp.where(inside[None, :], picked, jnp.zeros_like(picked))


def reference(courant, incident_prev, incident_now, wavelet, source_z, source_y, source_x, replica_seeds, receiver_z, receiver_y, receiver_x):
    speed_square = courant * courant
    history = [incident_prev, incident_now]
    for step_index in range(STEPS):
        current = history[-1]
        following = 2.0 * current - history[-2] + speed_square * laplace(jnp.pad(current, 4))
        following = inject(following, wavelet[step_index], source_z, source_y, source_x, 0, 0, 0)
        history.append(following)
    depth_coord = jnp.arange(NZ, dtype=jnp.int32)
    height_coord = jnp.arange(NY, dtype=jnp.int32)
    width_coord = jnp.arange(NX, dtype=jnp.int32)

    def one_replica(seed_value):
        contrast = perturbation(seed_value[None], depth_coord, height_coord, width_coord)[0]
        wave_prev = jnp.zeros(incident_now.shape, jnp.float32)
        wave_now = jnp.zeros(incident_now.shape, jnp.float32)
        recorded = []
        for step_index in range(STEPS):
            source_term = 2.0 * contrast * (history[step_index + 2] - 2.0 * history[step_index + 1] + history[step_index])
            wave_next = 2.0 * wave_now - wave_prev + speed_square * laplace(jnp.pad(wave_now, 4)) + source_term
            recorded.append(sample(wave_next[None], receiver_z, receiver_y, receiver_x, 0, 0)[0])
            wave_prev, wave_now = wave_now, wave_next
        return wave_now, jnp.stack(recorded)

    scattered_final, recorded = lax.map(one_replica, replica_seeds)
    traces = jnp.transpose(recorded, (1, 0, 2))
    return history[-1], scattered_final, traces
```

```python
import functools
import jax
import jax.numpy as jnp
from jax import lax
from jax.experimental import pallas as pl
from jax.experimental.pallas import tpu as pltpu
from jax.sharding import PartitionSpec as P

STEPS = 4
COEF = (-205.0 / 72.0, 8.0 / 5.0, -1.0 / 5.0, 8.0 / 315.0, -1.0 / 560.0)
MESH = pl.DeviceIdType.MESH
HI = lax.Precision.HIGHEST


def windowed(
    nslab,
    split,
    reach,
    win,
    wav_in,
    sz_in,
    sy_in,
    sx_in,
    seeds_in,
    rz_in,
    ry_in,
    rx_in,
    cour,
    prev_in,
    now_in,
    inc_out,
    wave_out,
    trace_out,
    U,
    C,
    W,
    K,
    INJ,
    XP,
    BAND,
    ROWS,
    TB,
    zu_s,
    zu_r,
    zc_s,
    zc_r,
    xu_s,
    xu_r,
    yc_s,
    yc_r,
    su_s,
    su_r,
    sc_s,
    sc_r,
    t_s,
    t_r,
    wav,
    sz,
    sy,
    sx,
    seeds,
    rz,
    ry,
    rx,
    in_s,
):
    cz, cy, pw = now_in.shape
    nx = cour.shape[2]
    ny = 2 * cy
    zw = win * cz
    nrec = trace_out.shape[2]
    half = nx // 2
    shot = lax.axis_index("shot")
    s = lax.axis_index("slab")
    b = lax.axis_index("rep")
    c = lax.axis_index("sub")

    def base_of(t):
        return jnp.clip(t - reach, 0, nslab - win)

    base = base_of(s)

    barrier = pltpu.get_barrier_semaphore()
    others = []
    for d in range(1, 2 * nslab):
        other = lax.rem(s * 2 + c + d, 2 * nslab)
        others.append(other)
        pl.semaphore_signal(
            barrier,
            inc=1,
            device_id={"slab": lax.div(other, 2), "sub": lax.rem(other, 2)},
            device_id_type=MESH,
        )
    pl.semaphore_signal(barrier, inc=1, device_id={"shot": 1 - shot}, device_id_type=MESH)
    greeted = 2 * nslab
    if split:
        pl.semaphore_signal(barrier, inc=1, device_id={"rep": 1 - b}, device_id_type=MESH)
        greeted += 1

    def zpos(t, of):
        return cz + (t - of) * cz

    def ypos(c_):
        return pl.multiple_of(8 + c_ * cy, 8)

    def xpos(h, width):
        return pl.multiple_of(h * width, 128)

    own_z = zpos(s, base)
    xown = pl.ds(xpos(b, pw), pw) if split else pl.ds(0, pw)
    fetch = [
        pltpu.make_async_copy(src, dst, in_s.at[i])
        for i, (src, dst) in enumerate(
            [
                (now_in, U.at[0, pl.ds(own_z, cz), pl.ds(ypos(c), cy), xown]),
                (prev_in, U.at[1, pl.ds(own_z, cz), pl.ds(ypos(c), cy), xown]),
                (cour, C.at[pl.ds(own_z, cz), pl.ds(pl.multiple_of(c * cy, 8), cy), :]),
                (seeds_in, seeds),
                (wav_in, wav),
                (sz_in, sz),
                (sy_in, sy),
                (sx_in, sx),
                (rz_in, rz),
                (ry_in, ry),
                (rx_in, rx),
            ]
        )
    ]
    for copy in fetch:
        copy.start()

    def u_piece(t, of, h):
        xs = pl.ds(xpos(h, pw), pw) if split else pl.ds(0, pw)
        return U.at[:, pl.ds(zpos(t, of), cz), pl.ds(ypos(c), cy), xs]

    def near(rows, c_):
        return pl.multiple_of((1 - c_) * (cy - rows), 8)

    def u_near(t, d, c_):
        rows = max(8, min(cy, -(-(16 - 4 * abs(d)) // 8) * 8))
        fields = pl.ds(0, 1 if abs(d) >= 3 else 2)
        return U.at[fields, pl.ds(zpos(t, base), cz), pl.ds(ypos(c_) + near(rows, c_), rows), :]

    def c_near(t, d, c_):
        rows = min(cy, -(-(12 - 4 * abs(d)) // 8) * 8)
        start = pl.multiple_of(c_ * cy, 8) + near(rows, c_)
        return C.at[pl.ds(zpos(t, base), cz), pl.ds(start, rows), :]

    def c_rows(t, of, c_, h):
        rows = pl.ds(pl.multiple_of(c_ * cy, 8), cy)
        xs = pl.ds(0, nx) if h is None else pl.ds(xpos(h, half), half)
        return C.at[pl.ds(zpos(t, of), cz), rows, xs]

    def rcopy(src, dst, ss, rs, device):
        return pltpu.make_async_remote_copy(
            src_ref=src, dst_ref=dst, send_sem=ss, recv_sem=rs, device_id=device, device_id_type=MESH
        )

    dists = []
    for d in range(reach, 0, -1):
        dists += [d, -d]

    for copy in fetch[:3]:
        copy.wait()
    pl.semaphore_wait(barrier, greeted)

    def z_copies(i, d):
        t = s + d
        of = base_of(t)
        return (
            rcopy(u_piece(s, base, b), u_piece(s, of, b), zu_s.at[i], zu_r.at[i], {"slab": t}),
            rcopy(
                c_rows(s, base, c, shot),
                c_rows(s, of, c, shot),
                zc_s.at[i],
                zc_r.at[i],
                {"slab": t},
            ),
        )

    def inside(t):
        return (t >= 0) & (t < nslab)

    def x_copy(i, t, h):
        return rcopy(u_piece(t, base, h), u_piece(t, base, h), xu_s.at[i], xu_r.at[i], {"rep": 1 - b})

    def y_copy(i, t, h):
        return rcopy(
            c_rows(t, base, c, h), c_rows(t, base, c, h), yc_s.at[i], yc_r.at[i], {"shot": 1 - shot}
        )

    def sub_u(i, t, d, mine):
        row = u_near(t, d, c if mine else 1 - c)
        return rcopy(row, row, su_s.at[i], su_r.at[i], {"sub": 1 - c})

    def sub_c(i, t, d, mine):
        row = c_near(t, d, c if mine else 1 - c)
        return rcopy(row, row, sc_s.at[i], sc_r.at[i], {"sub": 1 - c})

    if split:
        x_copy(0, s, b).start()
    for i, d in enumerate(dists):

        @pl.when(inside(s + d))
        def _():
            u_copy, c_copy = z_copies(i, d)
            u_copy.start()
            c_copy.start()

    sub_c(0, s, 0, True).start()

    wp = W.shape[-2]
    for buf in range(2):
        U[buf, pl.ds(0, cz)] = jnp.zeros((cz, wp, nx), jnp.float32)
        U[buf, pl.ds(cz + zw, cz)] = jnp.zeros((cz, wp, nx), jnp.float32)
        U[buf, pl.ds(cz, zw), pl.ds(0, 8), :] = jnp.zeros((zw, 8, nx), jnp.float32)
        U[buf, pl.ds(cz, zw), pl.ds(8 + ny, 8), :] = jnp.zeros((zw, 8, nx), jnp.float32)
        for r in range(2):
            W[buf, r, pl.ds(0, cz)] = jnp.zeros((cz, wp, nx), jnp.float32)
            W[buf, r, pl.ds(cz + zw, cz)] = jnp.zeros((cz, wp, nx), jnp.float32)
            W[buf, r, pl.ds(cz, zw), pl.ds(0, 8), :] = jnp.zeros((zw, 8, nx), jnp.float32)
            W[buf, r, pl.ds(cz, zw), pl.ds(8 + ny, 8), :] = jnp.zeros((zw, 8, nx), jnp.float32)

    gap = jnp.abs(
        lax.broadcasted_iota(jnp.int32, (nx, nx), 0) - lax.broadcasted_iota(jnp.int32, (nx, nx), 1)
    )
    band = jnp.zeros((nx, nx), jnp.float32)
    for k in range(1, 5):
        band = jnp.where(gap == k, COEF[k], band)
    high = band.astype(jnp.bfloat16)
    BAND[pl.ds(0, nx), :] = high
    BAND[pl.ds(nx, nx), :] = high
    BAND[pl.ds(2 * nx, nx), :] = (band - high.astype(jnp.float32)).astype(jnp.bfloat16)

    for copy in fetch[3:]:
        copy.wait()
    ycoord = lax.broadcasted_iota(jnp.int32, (ny, nx), 0)
    xcoord = lax.broadcasted_iota(jnp.int32, (ny, nx), 1)
    flat = ycoord * 19349663 + xcoord * 83492791

    @pl.loop(0, zw)
    def _(z):
        for r in range(2):
            h = flat + (seeds[r] * 668265263 + (base * cz + z) * 73856093)
            h = jnp.bitwise_xor(h, jnp.right_shift(h, 15))
            h = h * 1274126177
            h = jnp.bitwise_xor(h, jnp.right_shift(h, 13))
            f = jnp.bitwise_and(h, 65535).astype(jnp.float32)
            K[r, z] = f * (0.8 / 65535.0) - 0.4

    nsrc = sx.shape[0]
    lane = lax.broadcasted_iota(jnp.int32, (1, nsrc), 1)
    place = jnp.zeros((1, nsrc), jnp.int32)
    column = jnp.zeros((nsrc, nx), jnp.int32)
    ksub = lax.broadcasted_iota(jnp.int32, (nsrc, nx), 0)
    for k in range(nsrc):
        place = jnp.where(lane == k, (sz[k] - base * cz) * ny + sy[k], place)
        column = jnp.where(ksub == k, sx[k], column)
    hit_x = jnp.where(lax.broadcasted_iota(jnp.int32, (nsrc, nx), 1) == column, 1.0, 0.0)
    row_id = lax.broadcasted_iota(jnp.int32, (zw * ny, nsrc), 0)
    hit = row_id == place
    for n in range(STEPS):
        amounts = jnp.zeros((1, nsrc), jnp.float32)
        for k in range(nsrc):
            amounts = jnp.where(lane == k, wav[n, k], amounts)
        rows = jnp.where(hit, amounts, 0.0)
        INJ[n] = jnp.dot(rows, hit_x, precision=HI, preferred_element_type=jnp.float32).reshape(
            zw, ny, nx
        )

    def hand_over(i, d):
        @pl.when(inside(s - d))
        def _():
            t = s - d
            y_copy(i + 1, t, 1 - shot).wait_recv()
            if abs(d) < 3:
                sub_c(i + 1, t, d, True).start()
            if split:
                x_copy(i + 1, t, 1 - b).wait_recv()
            if abs(d) < 4:
                sub_u(i + 1, t, d, True).start()

    if split:
        x_copy(0, s, 1 - b).wait_recv()
    sub_u(0, s, 0, True).start()
    for i, d in enumerate(dists):

        @pl.when(inside(s - d))
        def _():
            t = s - d
            mine = u_piece(t, base, b)
            rcopy(mine, mine, zu_s.at[i], zu_r.at[i], {"slab": s}).wait_recv()
            if split:
                x_copy(i + 1, t, b).start()
            mine = c_rows(t, base, c, shot)
            rcopy(mine, mine, zc_s.at[i], zc_r.at[i], {"slab": s}).wait_recv()
            y_copy(i + 1, t, shot).start()

    for i, d in enumerate(dists):
        hand_over(i, d)

    sub_c(0, s, 0, False).wait_recv()
    sub_u(0, s, 0, False).wait_recv()
    for i, d in enumerate(dists):

        @pl.when(inside(s - d))
        def _():
            if abs(d) < 3:
                sub_c(i + 1, s - d, d, False).wait_recv()
            if abs(d) < 4:
                sub_u(i + 1, s - d, d, False).wait_recv()

    if split:
        x_copy(0, s, b).wait_send()
    sub_c(0, s, 0, True).wait_send()
    sub_u(0, s, 0, True).wait_send()
    for i, d in enumerate(dists):

        @pl.when(inside(s + d))
        def _():
            u_copy, c_copy = z_copies(i, d)
            u_copy.wait_send()
            c_copy.wait_send()

        @pl.when(inside(s - d))
        def _():
            t = s - d
            if split:
                x_copy(i + 1, t, b).wait_send()
            y_copy(i + 1, t, shot).wait_send()
            if abs(d) < 3:
                sub_c(i + 1, t, d, True).wait_send()
            if abs(d) < 4:
                sub_u(i + 1, t, d, True).wait_send()

    core = (s - base) * cz
    j0 = (s * 2 + c) * 4

    def step(n, y0, rows):
        now, before = n % 2, 1 - n % 2
        left = STEPS - 1 - n
        nz = min(zw, cz + 8 * left)
        z0 = jnp.clip(core - 4 * left, 0, zw - nz)
        wnow, wnext = (n + 1) % 2, n % 2
        ys = pl.ds(8 + y0, rows)
        yc = pl.ds(y0, rows)

        def across(ref):
            v = ref[pl.ds(cz + z0, nz), ys, :].reshape(nz * rows, nx)
            high = v.astype(jnp.bfloat16)
            low = (v - high.astype(jnp.float32)).astype(jnp.bfloat16)
            both = jnp.concatenate([high, low, high], axis=1)
            out = jnp.dot(both, BAND[...], preferred_element_type=jnp.float32)
            return out.reshape(nz, rows, nx)

        XP[0, pl.ds(0, nz), pl.ds(0, rows), :] = across(U.at[now])
        if n > 0:
            for r in range(2):
                XP[1 + r, pl.ds(0, nz), pl.ds(0, rows), :] = across(W.at[wnow, r])

        @pl.loop(0, nz, unroll=4)
        def _(i):
            z = z0 + i
            p = z + cz
            speed = C[p, yc, :]
            speed = speed * speed

            def lap(ref, mid, part):
                acc = part + (3.0 * COEF[0]) * mid
                for k in range(1, 5):
                    acc = acc + COEF[k] * (
                        (ref[p + k, ys, :] + ref[p - k, ys, :])
                        + (ref[p, pl.ds(8 + y0 + k, rows), :] + ref[p, pl.ds(8 + y0 - k, rows), :])
                    )
                return acc

            mid = U[now, p, ys, :]
            delta = speed * lap(U.at[now], mid, XP[0, i, pl.ds(0, rows), :]) + INJ[n, z, yc, :]
            U[before, p, ys, :] = 2.0 * mid - U[before, p, ys, :] + delta
            for r in range(2):
                term = K[r, z, yc, :] * delta
                if n > 0:
                    mid = W[wnow, r, p, ys, :]
                    term = term + speed * lap(W.at[wnow, r], mid, XP[1 + r, i, pl.ds(0, rows), :])
                    term = term + 2.0 * mid
                if n > 1:
                    term = term - W[wnext, r, p, ys, :]
                W[wnext, r, p, ys, :] = term

        for i in range(4):
            zj = rz[j0 + i] - base * cz + cz
            yj = ry[j0 + i] + 8
            for r in range(2):
                ROWS[pl.ds(i * 8 + n * 2 + r, 1), :] = W[wnext, r, zj, pl.ds(yj, 1), :]

    step(0, 0, ny)
    for side in range(2):

        @pl.when(c == side)
        def _():
            for n in range(1, STEPS):
                rows = min(ny, cy + 8 * -(-(STEPS - 1 - n) // 2))
                step(n, side * (ny - rows), rows)

    tw = TB.shape[2]
    lane_x = lax.broadcasted_iota(jnp.int32, (8, nx), 1)
    lane_j = lax.broadcasted_iota(jnp.int32, (8, tw), 1)
    tile = jnp.zeros((8, tw), jnp.float32)
    for i in range(4):
        picked = jnp.where(lane_x == rx[j0 + i], ROWS[pl.ds(i * 8, 8), :], 0.0)
        picked = jnp.sum(picked, axis=1, keepdims=True)
        tile = jnp.where(lane_j == j0 + i, picked, tile)
    me = s * 2 + c
    TB[me] = tile

    def t_copy(d, src, target):
        return rcopy(
            TB.at[src],
            TB.at[src],
            t_s.at[d],
            t_r.at[d],
            {"slab": lax.div(target, 2), "sub": lax.rem(target, 2)},
        )

    for d in range(1, 2 * nslab):
        t_copy(d, me, others[d - 1]).start()
    last = (STEPS - 1) % 2
    wave_out[...] = W[last, :, pl.ds(cz + core, cz), pl.ds(ypos(c), cy), :]
    if split:
        inc_out[...] = U[STEPS % 2, pl.ds(cz + core, cz), pl.ds(ypos(c), cy), xown]
    else:
        inc_out[...] = U[STEPS % 2, pl.ds(cz + core, cz), pl.ds(ypos(c), cy), :]

    for d in range(1, 2 * nslab):
        source = lax.rem(me + 2 * nslab - d, 2 * nslab)
        t_copy(d, source, others[d - 1]).wait_recv()
        tile = tile + TB[source]
    for d in range(1, 2 * nslab):
        t_copy(d, me, others[d - 1]).wait_send()
    for n in range(STEPS):
        trace_out[n] = tile[2 * n : 2 * n + 2, :nrec]


SCALE = 5040.0 / 4096.0
TAPS = tuple(v / 4096.0 for v in (-43050.0, 8064.0, -1008.0, 128.0, -9.0))


def tap_of(gap):
    out = jnp.where(gap == 1, TAPS[1], 0.0)
    for k in range(2, 5):
        out = jnp.where(gap == k, TAPS[k], out)
    return out


def gather(
    nslab,
    seeds_in,
    wav_in,
    sz_in,
    sy_in,
    sx_in,
    rz_in,
    ry_in,
    rx_in,
    cour,
    prev_in,
    now_in,
    U,
    C,
    K,
    INJ,
    A2,
    B2,
    G2,
    RX,
    RR,
    zu_s,
    zu_r,
    zc_s,
    zc_r,
    xu_s,
    xu_r,
    yc_s,
    yc_r,
    su_s,
    su_r,
    sc_s,
    sc_r,
    seeds,
    wav,
    sz,
    sy,
    sx,
    rz,
    ry,
    rx,
    in_s,
):
    cz, cy, pw = now_in.shape
    nz, ny, nx = C.shape
    size = nz * ny
    half = nx // 2
    shot = lax.axis_index("shot")
    s = lax.axis_index("slab")
    b = lax.axis_index("rep")
    c = lax.axis_index("sub")

    barrier = pltpu.get_barrier_semaphore()
    for d in range(1, nslab):
        pl.semaphore_signal(
            barrier, inc=1, device_id={"slab": lax.rem(s + d, nslab)}, device_id_type=MESH
        )
    for other in ({"shot": 1 - shot}, {"rep": 1 - b}, {"sub": 1 - c}):
        pl.semaphore_signal(barrier, inc=1, device_id=other, device_id_type=MESH)
    greeted = nslab + 2

    def rows_of(c_):
        return pl.ds(pl.multiple_of(c_ * cy, 8), cy)

    def lanes_of(h):
        return pl.ds(pl.multiple_of(h * half, 128), half)

    def u_at(t, c_, h):
        return U.at[:, pl.ds(t * cz, cz), rows_of(c_), lanes_of(h)]

    def u_full(t, c_):
        return U.at[:, pl.ds(t * cz, cz), rows_of(c_), :]

    def c_at(t, c_, h):
        return C.at[pl.ds(t * cz, cz), rows_of(c_), lanes_of(h)]

    def c_full(t, c_):
        return C.at[pl.ds(t * cz, cz), rows_of(c_), :]

    fetch = [
        pltpu.make_async_copy(src, dst, in_s.at[i])
        for i, (src, dst) in enumerate(
            [
                (now_in, U.at[0, pl.ds(s * cz, cz), rows_of(c), lanes_of(b)]),
                (prev_in, U.at[1, pl.ds(s * cz, cz), rows_of(c), lanes_of(b)]),
                (cour, c_full(s, c)),
                (seeds_in, seeds),
                (wav_in, wav),
                (sz_in, sz),
                (sy_in, sy),
                (sx_in, sx),
                (rz_in, rz),
                (ry_in, ry),
                (rx_in, rx),
            ]
        )
    ]
    for copy in fetch:
        copy.start()

    def rcopy(piece, ss, rs, device):
        return pltpu.make_async_remote_copy(
            src_ref=piece,
            dst_ref=piece,
            send_sem=ss,
            recv_sem=rs,
            device_id=device,
            device_id_type=MESH,
        )

    dists = []
    for d in range(nslab - 1, 0, -1):
        dists += [d, -d]

    def inside(t):
        return (t >= 0) & (t < nslab)

    def z_u(i, t, target):
        return rcopy(u_at(t, c, b), zu_s.at[i], zu_r.at[i], {"slab": target})

    def z_c(i, t, target):
        return rcopy(c_at(t, c, shot), zc_s.at[i], zc_r.at[i], {"slab": target})

    def x_u(i, t, h):
        return rcopy(u_at(t, c, h), xu_s.at[i], xu_r.at[i], {"rep": 1 - b})

    def y_c(i, t, h):
        return rcopy(c_at(t, c, h), yc_s.at[i], yc_r.at[i], {"shot": 1 - shot})

    def sub_u(i, t, c_):
        return rcopy(u_full(t, c_), su_s.at[i], su_r.at[i], {"sub": 1 - c})

    def sub_c(i, t, c_):
        return rcopy(c_full(t, c_), sc_s.at[i], sc_r.at[i], {"sub": 1 - c})

    for copy in fetch[:3]:
        copy.wait()
    pl.semaphore_wait(barrier, greeted)

    x_u(0, s, b).start()
    for i, d in enumerate(dists):

        @pl.when(inside(s + d))
        def _():
            z_u(i, s, s + d).start()
            z_c(i, s, s + d).start()

    sub_c(0, s, c).start()

    rowy = lax.broadcasted_iota(jnp.int32, (ny, size), 0)
    col = lax.broadcasted_iota(jnp.int32, (ny, size), 1)
    colz, coly = col // ny, col % ny

    @pl.loop(0, nz)
    def _(z):
        gap = jnp.where(
            rowy == coly, jnp.abs(z - colz), jnp.where(z == colz, jnp.abs(rowy - coly), 0)
        )
        taps = tap_of(gap).astype(jnp.bfloat16)
        zs = pl.ds(pl.multiple_of(z * ny, 16), ny)
        A2[zs, pl.ds(0, size)] = taps
        A2[zs, pl.ds(size, size)] = taps

    gap = jnp.abs(
        lax.broadcasted_iota(jnp.int32, (nx, nx), 0) - lax.broadcasted_iota(jnp.int32, (nx, nx), 1)
    )
    taps = tap_of(gap).astype(jnp.bfloat16)
    B2[pl.ds(0, nx), :] = taps
    B2[pl.ds(nx, nx), :] = taps

    for copy in fetch[3:]:
        copy.wait()
    ycoord = lax.broadcasted_iota(jnp.int32, (ny, nx), 0)
    xcoord = lax.broadcasted_iota(jnp.int32, (ny, nx), 1)
    flat = ycoord * 19349663 + xcoord * 83492791

    @pl.loop(0, nz)
    def _(z):
        for r in range(2):
            h = flat + (seeds[r] * 668265263 + z * 73856093)
            h = jnp.bitwise_xor(h, jnp.right_shift(h, 15))
            h = h * 1274126177
            h = jnp.bitwise_xor(h, jnp.right_shift(h, 13))
            f = jnp.bitwise_and(h, 65535).astype(jnp.float32)
            K[r, z] = f * (0.8 / 65535.0) - 0.4

    nsrc = sx.shape[0]
    lane = lax.broadcasted_iota(jnp.int32, (1, nsrc), 1)
    place = jnp.zeros((1, nsrc), jnp.int32)
    column = jnp.zeros((nsrc, nx), jnp.int32)
    ksub = lax.broadcasted_iota(jnp.int32, (nsrc, nx), 0)
    for k in range(nsrc):
        place = jnp.where(lane == k, sz[k] * ny + sy[k], place)
        column = jnp.where(ksub == k, sx[k], column)
    hit_x = jnp.where(lax.broadcasted_iota(jnp.int32, (nsrc, nx), 1) == column, 1.0, 0.0)
    hit = lax.broadcasted_iota(jnp.int32, (size, nsrc), 0) == place
    for n in range(STEPS):
        amounts = jnp.zeros((1, nsrc), jnp.float32)
        for k in range(nsrc):
            amounts = jnp.where(lane == k, wav[n, k], amounts)
        rows = jnp.where(hit, amounts, 0.0)
        INJ[n] = jnp.dot(rows, hit_x, precision=HI, preferred_element_type=jnp.float32).reshape(
            nz, ny, nx
        )

    nrec = rz.shape[0]
    sub_j = lax.broadcasted_iota(jnp.int32, (nrec, 128), 0)
    jz = jnp.zeros((nrec, 128), jnp.int32)
    jy = jnp.zeros((nrec, 128), jnp.int32)
    jx = jnp.zeros((nrec, 128), jnp.int32)
    for j in range(nrec):
        jz = jnp.where(sub_j == j, rz[j], jz)
        jy = jnp.where(sub_j == j, ry[j], jy)
        jx = jnp.where(sub_j == j, rx[j], jx)
    lane_j = lax.broadcasted_iota(jnp.int32, (nrec, 128), 1)
    for q in range(size // 128):
        z, y = (q * 128 + lane_j) // ny, (q * 128 + lane_j) % ny
        dz, dy = jnp.abs(z - jz), jnp.abs(y - jy)
        here = jnp.where(dz + dy == 0, 1.0, 0.0).astype(jnp.bfloat16)
        gap = jnp.where(dy == 0, dz, jnp.where(dz == 0, dy, 0))
        near = tap_of(gap).astype(jnp.bfloat16)
        for part in range(2):
            G2[pl.ds(0, nrec), pl.ds(part * size + q * 128, 128)] = here
            G2[pl.ds(nrec, nrec), pl.ds(part * size + q * 128, 128)] = near
    for q in range(nx // 128):
        gap = jnp.abs(q * 128 + lane_j - jx)
        RX[0, :, pl.ds(q * 128, 128)] = jnp.where(gap == 0, 1.0, 0.0)
        RX[1, :, pl.ds(q * 128, 128)] = tap_of(gap) + jnp.where(gap == 0, TAPS[0], 0.0)
    for j in range(nrec):
        for r in range(2):
            RR[r, pl.ds(j, 1), :] = K[r, rz[j], pl.ds(ry[j], 1), :]
        RR[2, pl.ds(j, 1), :] = INJ[STEPS - 1, rz[j], pl.ds(ry[j], 1), :]

    x_u(0, s, 1 - b).wait_recv()
    sub_u(0, s, c).start()
    for i, d in enumerate(dists):

        @pl.when(inside(s - d))
        def _():
            z_u(i, s - d, s).wait_recv()
            x_u(i + 1, s - d, b).start()
            z_c(i, s - d, s).wait_recv()
            y_c(i + 1, s - d, shot).start()

    for i, d in enumerate(dists):

        @pl.when(inside(s - d))
        def _():
            y_c(i + 1, s - d, 1 - shot).wait_recv()
            sub_c(i + 1, s - d, c).start()
            x_u(i + 1, s - d, 1 - b).wait_recv()
            sub_u(i + 1, s - d, c).start()

    sub_c(0, s, 1 - c).wait_recv()
    sub_u(0, s, 1 - c).wait_recv()
    for i, d in enumerate(dists):

        @pl.when(inside(s - d))
        def _():
            sub_c(i + 1, s - d, 1 - c).wait_recv()
            sub_u(i + 1, s - d, 1 - c).wait_recv()

    x_u(0, s, b).wait_send()
    sub_c(0, s, c).wait_send()
    sub_u(0, s, c).wait_send()
    for i, d in enumerate(dists):

        @pl.when(inside(s + d))
        def _():
            z_u(i, s, s + d).wait_send()
            z_c(i, s, s + d).wait_send()

        @pl.when(inside(s - d))
        def _():
            x_u(i + 1, s - d, b).wait_send()
            y_c(i + 1, s - d, shot).wait_send()
            sub_c(i + 1, s - d, c).wait_send()
            sub_u(i + 1, s - d, c).wait_send()


def advance(
    rz_in,
    ry_in,
    U0,
    C,
    K,
    INJ,
    A2,
    B2,
    G2,
    RX,
    RR,
    inc_out,
    wave_out,
    trace_out,
    U,
    W,
    HL,
    LAP,
    SP,
    INC,
    WAVE,
    TR,
    RC,
    rz,
    ry,
    in_s,
    out_s,
):
    cz, cy, pw = inc_out.shape
    nz, ny, nx = C.shape
    size = nz * ny
    nrec = rz.shape[0]
    s = lax.axis_index("slab")
    b = lax.axis_index("rep")
    c = lax.axis_index("sub")
    fetch = [
        pltpu.make_async_copy(src, dst, in_s.at[i])
        for i, (src, dst) in enumerate([(rz_in, rz), (ry_in, ry)])
    ]
    for copy in fetch:
        copy.start()

    def split(field, z, v):
        high = v.astype(jnp.bfloat16)
        HL[0, z, :, pl.ds(field * nx, nx)] = high
        HL[1, z, :, pl.ds(field * nx, nx)] = (v - high.astype(jnp.float32)).astype(jnp.bfloat16)

    def parts(field):
        xs = pl.ds(field * nx, nx)
        return HL[0, :, :, xs].reshape(size, nx), HL[1, :, :, xs].reshape(size, nx)

    def lap_all(field):
        high, low = parts(field)
        lhs = jnp.concatenate([A2[...], high, low], axis=1)
        rhs = jnp.concatenate([high, low, B2[...]], axis=0)
        LAP[field] = jnp.dot(lhs, rhs, preferred_element_type=jnp.float32).reshape(nz, ny, nx)

    def at_receivers(field, rows):
        high, low = parts(field)
        rhs = jnp.concatenate([high, low], axis=0)
        return jnp.dot(G2[pl.ds(0, rows), :], rhs, preferred_element_type=jnp.float32)

    def pick(rows):
        return jnp.sum(rows, axis=1, keepdims=True)

    @pl.loop(0, nz, unroll=2)
    def _(z):
        split(0, z, U0[0, z])
        SP[z] = C[z] * C[z] * (1.0 / SCALE)

    seen = {}
    for n in range(STEPS - 1):
        now, before = n % 2, 1 - n % 2
        lap_all(0)
        if n > 0:
            for r in range(2):
                lap_all(1 + r)
                seen[n, r] = pick(at_receivers(1 + r, nrec) * RX[0])
        wnow, wnext = (n + 1) % 2, n % 2

        @pl.loop(0, nz, unroll=2)
        def _(z):
            speed = SP[z]
            unow = U0 if n == 0 else U
            uold = U0 if n < 2 else U
            mid = unow[now, z]
            delta = speed * (LAP[0, z] + TAPS[0] * mid) + INJ[n, z]
            v = 2.0 * mid - uold[before, z] + delta
            U[before, z] = v
            split(0, z, v)
            for r in range(2):
                v = K[r, z] * delta
                if n > 0:
                    mid = W[wnow, r, z]
                    v = v + (speed * (LAP[1 + r, z] + TAPS[0] * mid) + 2.0 * mid)
                if n > 1:
                    v = v - W[wnext, r, z]
                W[wnext, r, z] = v
                split(1 + r, z, v)

    for copy in fetch:
        copy.wait()
    for j in range(nrec):
        RC[pl.ds(j, 1), :] = SP[rz[j], pl.ds(ry[j], 1), :]

    n = STEPS - 1
    now, before = n % 2, 1 - n % 2
    wnow, wnext = (n + 1) % 2, n % 2
    own_z = pl.ds(s * cz, cz)
    own_y = pl.ds(pl.multiple_of(c * cy, 16), cy)
    lanes = pl.ds(pl.multiple_of(b * pw, 128), pw)
    area = cz * cy

    def own(ref, *lead):
        return ref[(*lead, own_z, own_y, slice(None))].reshape(area, nx)

    first = pl.multiple_of(s * cz * ny + c * cy, 16)
    own_a = jnp.concatenate(
        [A2[pl.ds(pl.multiple_of(first + z * ny, 16), cy), :] for z in range(cz)], axis=0
    )
    speed = own(SP)
    speed_j = pick(RC[...] * RX[0])

    def last(field, mid):
        high, low = parts(field)
        xs = pl.ds(field * nx, nx)
        mine = [HL[p, own_z, own_y, xs].reshape(area, nx) for p in range(2)]
        lhs = jnp.concatenate([own_a, G2[...]], axis=0)
        out = jnp.dot(
            lhs, jnp.concatenate([high, low], axis=0), preferred_element_type=jnp.float32
        )
        across = jnp.dot(
            jnp.concatenate(mine, axis=1), B2[...], preferred_element_type=jnp.float32
        )
        here = out[area : area + nrec]
        lap_j = pick(out[area + nrec :] * RX[0] + here * RX[1])
        return out[:area] + across + TAPS[0] * mid, pick(here * RX[0]), lap_j

    mid = own(U, now)
    lap, _, lap_j = last(0, mid)
    delta = speed * lap + own(INJ, n)
    INC[...] = (2.0 * mid - own(U, before) + delta).reshape(cz, cy, nx)
    outs = [pltpu.make_async_copy(INC.at[:, :, lanes], inc_out, out_s.at[0])]
    outs[0].start()
    delta_j = speed_j * lap_j + pick(RR[2] * RX[0])
    for r in range(2):
        mid = own(W, wnow, r)
        lap, here, lap_j = last(1 + r, mid)
        v = own(K, r) * delta + speed * lap + 2.0 * mid - own(W, wnext, r)
        WAVE[r] = v.reshape(cz, cy, nx)
        outs.append(pltpu.make_async_copy(WAVE.at[r], wave_out.at[r], out_s.at[1 + r]))
        outs[-1].start()
        seen[n, r] = here
        kick = pick(RR[r] * RX[0]) * delta_j
        seen[n + 1, r] = 2.0 * here - seen[n - 1, r] + speed_j * lap_j + kick
    lane = lax.broadcasted_iota(jnp.int32, (nrec, 128), 1)
    table = jnp.zeros((nrec, 128), jnp.float32)
    for n in range(STEPS):
        for r in range(2):
            table = jnp.where(lane == 2 * n + r, seen[n + 1, r], table)
    table = table.T
    for n in range(STEPS):
        TR[n] = table[2 * n : 2 * n + 2, :nrec]
    outs.append(pltpu.make_async_copy(TR, trace_out, out_s.at[3]))
    outs[-1].start()
    for copy in outs:
        copy.wait()


def whole(nslab, courant, prev, now, wavelet, sz, sy, sx, seeds, rz, ry, rx):
    cz, cy, pw = now.shape
    nx = courant.shape[2]
    nz, ny = nslab * cz, 2 * cy
    size = nz * ny
    nrec = rz.shape[0]
    nd = 2 * (nslab - 1)
    hbm = pl.BlockSpec(memory_space=pltpu.HBM)
    vmem = pl.BlockSpec(memory_space=pltpu.VMEM)
    f32, bf16 = jnp.float32, jnp.bfloat16
    dma = pltpu.SemaphoreType.DMA
    fixed = [
        pltpu.with_memory_space_constraint(a, pltpu.HBM)
        for a in (seeds, wavelet, sz, sy, sx, rz, ry, rx, courant, prev, now)
    ]
    held = pl.pallas_call(
        functools.partial(gather, nslab),
        out_shape=(
            pltpu.VMEM((2, nz, ny, nx), f32),
            pltpu.VMEM((nz, ny, nx), f32),
            pltpu.VMEM((2, nz, ny, nx), f32),
            pltpu.VMEM((STEPS, nz, ny, nx), f32),
            pltpu.VMEM((size, 2 * size), bf16),
            pltpu.VMEM((2 * nx, nx), bf16),
            pltpu.VMEM((2 * nrec, 2 * size), bf16),
            pltpu.VMEM((2, nrec, nx), f32),
            pltpu.VMEM((3, nrec, nx), f32),
        ),
        in_specs=[hbm] * 11,
        out_specs=(vmem,) * 9,
        scratch_shapes=[dma((nd,))] * 4
        + [dma((nd + 1,))] * 8
        + [pltpu.SMEM(a.shape, a.dtype) for a in (seeds, wavelet, sz, sy, sx, rz, ry, rx)]
        + [dma((11,))],
        compiler_params=pltpu.CompilerParams(
            collective_id=0, has_side_effects=True, vmem_limit_bytes=56 << 20
        ),
    )(*fixed)
    return pl.pallas_call(
        functools.partial(advance),
        out_shape=(
            jax.ShapeDtypeStruct((cz, cy, pw), f32),
            jax.ShapeDtypeStruct((2, cz, cy, nx), f32),
            jax.ShapeDtypeStruct((STEPS, 2, nrec), f32),
        ),
        in_specs=[hbm] * 2 + [vmem] * 9,
        out_specs=(hbm,) * 3,
        scratch_shapes=[
            pltpu.VMEM((2, nz, ny, nx), f32),
            pltpu.VMEM((2, 2, nz, ny, nx), f32),
            pltpu.VMEM((2, nz, ny, 3 * nx), bf16),
            pltpu.VMEM((3, nz, ny, nx), f32),
            pltpu.VMEM((nz, ny, nx), f32),
            pltpu.VMEM((cz, cy, nx), f32),
            pltpu.VMEM((2, cz, cy, nx), f32),
            pltpu.VMEM((STEPS, 2, nrec), f32),
            pltpu.VMEM((nrec, nx), f32),
            pltpu.SMEM(rz.shape, rz.dtype),
            pltpu.SMEM(ry.shape, ry.dtype),
            dma((2,)),
            dma((4,)),
        ],
        compiler_params=pltpu.CompilerParams(vmem_limit_bytes=32 << 20),
    )(fixed[5], fixed[6], *held)


def solution(mesh):
    nslab = mesh.shape["slab"]
    reach = min(4, nslab - 1)
    win = min(nslab, 9)

    def shards(courant, prev, now, wavelet, sz, sy, sx, seeds, rz, ry, rx):
        cz, cy, pw = now.shape
        nx = courant.shape[2]
        split = 2 * pw == nx and pw % 128 == 0
        if split and nslab <= 4 and cy % 16 == 0:
            return whole(nslab, courant, prev, now, wavelet, sz, sy, sx, seeds, rz, ry, rx)
        if not split:
            prev = lax.all_gather(prev, "rep", axis=2, tiled=True)
            now = lax.all_gather(now, "rep", axis=2, tiled=True)
        width = now.shape[2]
        ny = 2 * cy
        zw = win * cz
        nd = 2 * reach
        nrec = rz.shape[0]
        tw = -(-nrec // 128) * 128
        group = 2 * nslab
        hbm = pl.BlockSpec(memory_space=pltpu.HBM)
        vmem = pl.BlockSpec(memory_space=pltpu.VMEM)
        f32 = jnp.float32
        dma = pltpu.SemaphoreType.DMA
        inc, wave, traces = pl.pallas_call(
            functools.partial(windowed, nslab, split, reach, win),
            out_shape=(
                pltpu.VMEM((cz, cy, width), f32),
                pltpu.VMEM((2, cz, cy, nx), f32),
                pltpu.VMEM((STEPS, 2, nrec), f32),
            ),
            in_specs=[hbm] * 11,
            out_specs=(vmem, vmem, vmem),
            scratch_shapes=[
                pltpu.VMEM((2, zw + 2 * cz, ny + 16, nx), f32),
                pltpu.VMEM((zw + 2 * cz, ny, nx), f32),
                pltpu.VMEM((2, 2, zw + 2 * cz, ny + 16, nx), f32),
                pltpu.VMEM((2, zw, ny, nx), f32),
                pltpu.VMEM((STEPS, zw, ny, nx), f32),
                pltpu.VMEM((3, zw, ny, nx), f32),
                pltpu.VMEM((3 * nx, nx), jnp.bfloat16),
                pltpu.VMEM((32, nx), f32),
                pltpu.VMEM((group, 8, tw), f32),
            ]
            + [dma((nd,))] * 4
            + [dma((nd + 1,))] * 8
            + [dma((group,))] * 2
            + [pltpu.SMEM(a.shape, a.dtype) for a in (wavelet, sz, sy, sx, seeds, rz, ry, rx)]
            + [dma((11,))],
            compiler_params=pltpu.CompilerParams(
                collective_id=0, has_side_effects=True, vmem_limit_bytes=60 << 20
            ),
        )(wavelet, sz, sy, sx, seeds, rz, ry, rx, courant, prev, now)
        if not split:
            pw0 = width // lax.axis_size("rep")
            inc = lax.dynamic_slice_in_dim(inc, lax.axis_index("rep") * pw0, pw0, 2)
        return inc, wave, traces

    return jax.shard_map(
        shards,
        mesh=mesh,
        in_specs=(
            P("slab", "sub", None),
            P(("shot", "slab"), "sub", "rep"),
            P(("shot", "slab"), "sub", "rep"),
            P(),
            P("shot"),
            P("shot"),
            P("shot"),
            P("rep"),
            P(),
            P(),
            P(),
        ),
        out_specs=(
            P(("shot", "slab"), "sub", "rep"),
            P("rep", ("shot", "slab"), "sub", None),
            P("shot", "rep", None),
        ),
        check_vma=False,
    )
```

```python
import functools
import jax
import jax.numpy as jnp
from jax import lax
from jax.experimental import pallas as pl
from jax.experimental.pallas import tpu as pltpu
from jax.sharding import PartitionSpec as P

STEPS = 4
COEF = (-205.0 / 72.0, 8.0 / 5.0, -1.0 / 5.0, 8.0 / 315.0, -1.0 / 560.0)
MESH = pl.DeviceIdType.MESH
HI = lax.Precision.HIGHEST


def windowed(
    nslab,
    split,
    reach,
    win,
    wav_in,
    sz_in,
    sy_in,
    sx_in,
    seeds_in,
    rz_in,
    ry_in,
    rx_in,
    cour,
    prev_in,
    now_in,
    inc_out,
    wave_out,
    trace_out,
    U,
    C,
    W,
    K,
    INJ,
    XP,
    BAND,
    ROWS,
    TB,
    zu_s,
    zu_r,
    zc_s,
    zc_r,
    xu_s,
    xu_r,
    yc_s,
    yc_r,
    su_s,
    su_r,
    sc_s,
    sc_r,
    t_s,
    t_r,
    wav,
    sz,
    sy,
    sx,
    seeds,
    rz,
    ry,
    rx,
    in_s,
):
    cz, cy, pw = now_in.shape
    nx = cour.shape[2]
    ny = 2 * cy
    zw = win * cz
    nrec = trace_out.shape[2]
    half = nx // 2
    shot = lax.axis_index("shot")
    s = lax.axis_index("slab")
    b = lax.axis_index("rep")
    c = lax.axis_index("sub")

    def base_of(t):
        return jnp.clip(t - reach, 0, nslab - win)

    base = base_of(s)

    barrier = pltpu.get_barrier_semaphore()
    others = []
    for d in range(1, 2 * nslab):
        other = lax.rem(s * 2 + c + d, 2 * nslab)
        others.append(other)
        pl.semaphore_signal(
            barrier,
            inc=1,
            device_id={"slab": lax.div(other, 2), "sub": lax.rem(other, 2)},
            device_id_type=MESH,
        )
    pl.semaphore_signal(barrier, inc=1, device_id={"shot": 1 - shot}, device_id_type=MESH)
    greeted = 2 * nslab
    if split:
        pl.semaphore_signal(barrier, inc=1, device_id={"rep": 1 - b}, device_id_type=MESH)
        greeted += 1

    def zpos(t, of):
        return cz + (t - of) * cz

    def ypos(c_):
        return pl.multiple_of(8 + c_ * cy, 8)

    def xpos(h, width):
        return pl.multiple_of(h * width, 128)

    own_z = zpos(s, base)
    xown = pl.ds(xpos(b, pw), pw) if split else pl.ds(0, pw)
    fetch = [
        pltpu.make_async_copy(src, dst, in_s.at[i])
        for i, (src, dst) in enumerate(
            [
                (now_in, U.at[0, pl.ds(own_z, cz), pl.ds(ypos(c), cy), xown]),
                (prev_in, U.at[1, pl.ds(own_z, cz), pl.ds(ypos(c), cy), xown]),
                (cour, C.at[pl.ds(own_z, cz), pl.ds(pl.multiple_of(c * cy, 8), cy), :]),
                (seeds_in, seeds),
                (wav_in, wav),
                (sz_in, sz),
                (sy_in, sy),
                (sx_in, sx),
                (rz_in, rz),
                (ry_in, ry),
                (rx_in, rx),
            ]
        )
    ]
    for copy in fetch:
        copy.start()

    def u_piece(t, of, h):
        xs = pl.ds(xpos(h, pw), pw) if split else pl.ds(0, pw)
        return U.at[:, pl.ds(zpos(t, of), cz), pl.ds(ypos(c), cy), xs]

    def near(rows, c_):
        return pl.multiple_of((1 - c_) * (cy - rows), 8)

    def u_near(t, d, c_):
        rows = max(8, min(cy, -(-(16 - 4 * abs(d)) // 8) * 8))
        fields = pl.ds(0, 1 if abs(d) >= 3 else 2)
        return U.at[fields, pl.ds(zpos(t, base), cz), pl.ds(ypos(c_) + near(rows, c_), rows), :]

    def c_near(t, d, c_):
        rows = min(cy, -(-(12 - 4 * abs(d)) // 8) * 8)
        start = pl.multiple_of(c_ * cy, 8) + near(rows, c_)
        return C.at[pl.ds(zpos(t, base), cz), pl.ds(start, rows), :]

    def c_rows(t, of, c_, h):
        rows = pl.ds(pl.multiple_of(c_ * cy, 8), cy)
        xs = pl.ds(0, nx) if h is None else pl.ds(xpos(h, half), half)
        return C.at[pl.ds(zpos(t, of), cz), rows, xs]

    def rcopy(src, dst, ss, rs, device):
        return pltpu.make_async_remote_copy(
            src_ref=src, dst_ref=dst, send_sem=ss, recv_sem=rs, device_id=device, device_id_type=MESH
        )

    dists = []
    for d in range(reach, 0, -1):
        dists += [d, -d]

    for copy in fetch[:3]:
        copy.wait()
    pl.semaphore_wait(barrier, greeted)

    def z_copies(i, d):
        t = s + d
        of = base_of(t)
        return (
            rcopy(u_piece(s, base, b), u_piece(s, of, b), zu_s.at[i], zu_r.at[i], {"slab": t}),
            rcopy(
                c_rows(s, base, c, shot),
                c_rows(s, of, c, shot),
                zc_s.at[i],
                zc_r.at[i],
                {"slab": t},
            ),
        )

    def inside(t):
        return (t >= 0) & (t < nslab)

    def x_copy(i, t, h):
        return rcopy(u_piece(t, base, h), u_piece(t, base, h), xu_s.at[i], xu_r.at[i], {"rep": 1 - b})

    def y_copy(i, t, h):
        return rcopy(
            c_rows(t, base, c, h), c_rows(t, base, c, h), yc_s.at[i], yc_r.at[i], {"shot": 1 - shot}
        )

    def sub_u(i, t, d, mine):
        row = u_near(t, d, c if mine else 1 - c)
        return rcopy(row, row, su_s.at[i], su_r.at[i], {"sub": 1 - c})

    def sub_c(i, t, d, mine):
        row = c_near(t, d, c if mine else 1 - c)
        return rcopy(row, row, sc_s.at[i], sc_r.at[i], {"sub": 1 - c})

    if split:
        x_copy(0, s, b).start()
    for i, d in enumerate(dists):

        @pl.when(inside(s + d))
        def _():
            u_copy, c_copy = z_copies(i, d)
            u_copy.start()
            c_copy.start()

    sub_c(0, s, 0, True).start()

    wp = W.shape[-2]
    for buf in range(2):
        U[buf, pl.ds(0, cz)] = jnp.zeros((cz, wp, nx), jnp.float32)
        U[buf, pl.ds(cz + zw, cz)] = jnp.zeros((cz, wp, nx), jnp.float32)
        U[buf, pl.ds(cz, zw), pl.ds(0, 8), :] = jnp.zeros((zw, 8, nx), jnp.float32)
        U[buf, pl.ds(cz, zw), pl.ds(8 + ny, 8), :] = jnp.zeros((zw, 8, nx), jnp.float32)
        for r in range(2):
            W[buf, r, pl.ds(0, cz)] = jnp.zeros((cz, wp, nx), jnp.float32)
            W[buf, r, pl.ds(cz + zw, cz)] = jnp.zeros((cz, wp, nx), jnp.float32)
            W[buf, r, pl.ds(cz, zw), pl.ds(0, 8), :] = jnp.zeros((zw, 8, nx), jnp.float32)
            W[buf, r, pl.ds(cz, zw), pl.ds(8 + ny, 8), :] = jnp.zeros((zw, 8, nx), jnp.float32)

    gap = jnp.abs(
        lax.broadcasted_iota(jnp.int32, (nx, nx), 0) - lax.broadcasted_iota(jnp.int32, (nx, nx), 1)
    )
    band = jnp.zeros((nx, nx), jnp.float32)
    for k in range(1, 5):
        band = jnp.where(gap == k, COEF[k], band)
    high = band.astype(jnp.bfloat16)
    BAND[pl.ds(0, nx), :] = high
    BAND[pl.ds(nx, nx), :] = high
    BAND[pl.ds(2 * nx, nx), :] = (band - high.astype(jnp.float32)).astype(jnp.bfloat16)

    for copy in fetch[3:]:
        copy.wait()
    ycoord = lax.broadcasted_iota(jnp.int32, (ny, nx), 0)
    xcoord = lax.broadcasted_iota(jnp.int32, (ny, nx), 1)
    flat = ycoord * 19349663 + xcoord * 83492791

    @pl.loop(0, zw)
    def _(z):
        for r in range(2):
            h = flat + (seeds[r] * 668265263 + (base * cz + z) * 73856093)
            h = jnp.bitwise_xor(h, jnp.right_shift(h, 15))
            h = h * 1274126177
            h = jnp.bitwise_xor(h, jnp.right_shift(h, 13))
            f = jnp.bitwise_and(h, 65535).astype(jnp.float32)
            K[r, z] = f * (0.8 / 65535.0) - 0.4

    nsrc = sx.shape[0]
    lane = lax.broadcasted_iota(jnp.int32, (1, nsrc), 1)
    place = jnp.zeros((1, nsrc), jnp.int32)
    column = jnp.zeros((nsrc, nx), jnp.int32)
    ksub = lax.broadcasted_iota(jnp.int32, (nsrc, nx), 0)
    for k in range(nsrc):
        place = jnp.where(lane == k, (sz[k] - base * cz) * ny + sy[k], place)
        column = jnp.where(ksub == k, sx[k], column)
    hit_x = jnp.where(lax.broadcasted_iota(jnp.int32, (nsrc, nx), 1) == column, 1.0, 0.0)
    row_id = lax.broadcasted_iota(jnp.int32, (zw * ny, nsrc), 0)
    hit = row_id == place
    for n in range(STEPS):
        amounts = jnp.zeros((1, nsrc), jnp.float32)
        for k in range(nsrc):
            amounts = jnp.where(lane == k, wav[n, k], amounts)
        rows = jnp.where(hit, amounts, 0.0)
        INJ[n] = jnp.dot(rows, hit_x, precision=HI, preferred_element_type=jnp.float32).reshape(
            zw, ny, nx
        )

    def hand_over(i, d):
        @pl.when(inside(s - d))
        def _():
            t = s - d
            y_copy(i + 1, t, 1 - shot).wait_recv()
            if abs(d) < 3:
                sub_c(i + 1, t, d, True).start()
            if split:
                x_copy(i + 1, t, 1 - b).wait_recv()
            if abs(d) < 4:
                sub_u(i + 1, t, d, True).start()

    if split:
        x_copy(0, s, 1 - b).wait_recv()
    sub_u(0, s, 0, True).start()
    for i, d in enumerate(dists):

        @pl.when(inside(s - d))
        def _():
            t = s - d
            mine = u_piece(t, base, b)
            rcopy(mine, mine, zu_s.at[i], zu_r.at[i], {"slab": s}).wait_recv()
            if split:
                x_copy(i + 1, t, b).start()
            mine = c_rows(t, base, c, shot)
            rcopy(mine, mine, zc_s.at[i], zc_r.at[i], {"slab": s}).wait_recv()
            y_copy(i + 1, t, shot).start()

    for i, d in enumerate(dists):
        hand_over(i, d)

    sub_c(0, s, 0, False).wait_recv()
    sub_u(0, s, 0, False).wait_recv()
    for i, d in enumerate(dists):

        @pl.when(inside(s - d))
        def _():
            if abs(d) < 3:
                sub_c(i + 1, s - d, d, False).wait_recv()
            if abs(d) < 4:
                sub_u(i + 1, s - d, d, False).wait_recv()

    if split:
        x_copy(0, s, b).wait_send()
    sub_c(0, s, 0, True).wait_send()
    sub_u(0, s, 0, True).wait_send()
    for i, d in enumerate(dists):

        @pl.when(inside(s + d))
        def _():
            u_copy, c_copy = z_copies(i, d)
            u_copy.wait_send()
            c_copy.wait_send()

        @pl.when(inside(s - d))
        def _():
            t = s - d
            if split:
                x_copy(i + 1, t, b).wait_send()
            y_copy(i + 1, t, shot).wait_send()
            if abs(d) < 3:
                sub_c(i + 1, t, d, True).wait_send()
            if abs(d) < 4:
                sub_u(i + 1, t, d, True).wait_send()

    core = (s - base) * cz
    j0 = (s * 2 + c) * 4

    def step(n, y0, rows):
        now, before = n % 2, 1 - n % 2
        left = STEPS - 1 - n
        nz = min(zw, cz + 8 * left)
        z0 = jnp.clip(core - 4 * left, 0, zw - nz)
        wnow, wnext = (n + 1) % 2, n % 2
        ys = pl.ds(8 + y0, rows)
        yc = pl.ds(y0, rows)

        def across(ref):
            v = ref[pl.ds(cz + z0, nz), ys, :].reshape(nz * rows, nx)
            high = v.astype(jnp.bfloat16)
            low = (v - high.astype(jnp.float32)).astype(jnp.bfloat16)
            both = jnp.concatenate([high, low, high], axis=1)
            out = jnp.dot(both, BAND[...], preferred_element_type=jnp.float32)
            return out.reshape(nz, rows, nx)

        XP[0, pl.ds(0, nz), pl.ds(0, rows), :] = across(U.at[now])
        if n > 0:
            for r in range(2):
                XP[1 + r, pl.ds(0, nz), pl.ds(0, rows), :] = across(W.at[wnow, r])

        @pl.loop(0, nz, unroll=4)
        def _(i):
            z = z0 + i
            p = z + cz
            speed = C[p, yc, :]
            speed = speed * speed

            def lap(ref, mid, part):
                acc = part + (3.0 * COEF[0]) * mid
                for k in range(1, 5):
                    acc = acc + COEF[k] * (
                        (ref[p + k, ys, :] + ref[p - k, ys, :])
                        + (ref[p, pl.ds(8 + y0 + k, rows), :] + ref[p, pl.ds(8 + y0 - k, rows), :])
                    )
                return acc

            mid = U[now, p, ys, :]
            delta = speed * lap(U.at[now], mid, XP[0, i, pl.ds(0, rows), :]) + INJ[n, z, yc, :]
            U[before, p, ys, :] = 2.0 * mid - U[before, p, ys, :] + delta
            for r in range(2):
                term = K[r, z, yc, :] * delta
                if n > 0:
                    mid = W[wnow, r, p, ys, :]
                    term = term + speed * lap(W.at[wnow, r], mid, XP[1 + r, i, pl.ds(0, rows), :])
                    term = term + 2.0 * mid
                if n > 1:
                    term = term - W[wnext, r, p, ys, :]
                W[wnext, r, p, ys, :] = term

        for i in range(4):
            zj = rz[j0 + i] - base * cz + cz
            yj = ry[j0 + i] + 8
            for r in range(2):
                ROWS[pl.ds(i * 8 + n * 2 + r, 1), :] = W[wnext, r, zj, pl.ds(yj, 1), :]

    step(0, 0, ny)
    for side in range(2):

        @pl.when(c == side)
        def _():
            for n in range(1, STEPS):
                rows = min(ny, cy + 8 * -(-(STEPS - 1 - n) // 2))
                step(n, side * (ny - rows), rows)

    tw = TB.shape[2]
    lane_x = lax.broadcasted_iota(jnp.int32, (8, nx), 1)
    lane_j = lax.broadcasted_iota(jnp.int32, (8, tw), 1)
    tile = jnp.zeros((8, tw), jnp.float32)
    for i in range(4):
        picked = jnp.where(lane_x == rx[j0 + i], ROWS[pl.ds(i * 8, 8), :], 0.0)
        picked = jnp.sum(picked, axis=1, keepdims=True)
        tile = jnp.where(lane_j == j0 + i, picked, tile)
    me = s * 2 + c
    TB[me] = tile

    def t_copy(d, src, target):
        return rcopy(
            TB.at[src],
            TB.at[src],
            t_s.at[d],
            t_r.at[d],
            {"slab": lax.div(target, 2), "sub": lax.rem(target, 2)},
        )

    for d in range(1, 2 * nslab):
        t_copy(d, me, others[d - 1]).start()
    last = (STEPS - 1) % 2
    wave_out[...] = W[last, :, pl.ds(cz + core, cz), pl.ds(ypos(c), cy), :]
    if split:
        inc_out[...] = U[STEPS % 2, pl.ds(cz + core, cz), pl.ds(ypos(c), cy), xown]
    else:
        inc_out[...] = U[STEPS % 2, pl.ds(cz + core, cz), pl.ds(ypos(c), cy), :]

    for d in range(1, 2 * nslab):
        source = lax.rem(me + 2 * nslab - d, 2 * nslab)
        t_copy(d, source, others[d - 1]).wait_recv()
        tile = tile + TB[source]
    for d in range(1, 2 * nslab):
        t_copy(d, me, others[d - 1]).wait_send()
    for n in range(STEPS):
        trace_out[n] = tile[2 * n : 2 * n + 2, :nrec]


SCALE = 5040.0 / 4096.0
TAPS = tuple(v / 4096.0 for v in (-43050.0, 8064.0, -1008.0, 128.0, -9.0))


def tap_of(gap):
    out = jnp.where(gap == 1, TAPS[1], 0.0)
    for k in range(2, 5):
        out = jnp.where(gap == k, TAPS[k], out)
    return out


def gather(
    nslab,
    seeds_in,
    wav_in,
    sz_in,
    sy_in,
    sx_in,
    rz_in,
    ry_in,
    rx_in,
    cour,
    prev_in,
    now_in,
    U,
    C,
    K,
    INJ,
    A,
    B2,
    G2,
    RX,
    RR,
    zu_s,
    zu_r,
    zc_s,
    zc_r,
    xu_s,
    xu_r,
    yc_s,
    yc_r,
    su_s,
    su_r,
    sc_s,
    sc_r,
    seeds,
    wav,
    sz,
    sy,
    sx,
    rz,
    ry,
    rx,
    in_s,
):
    cz, cy, pw = now_in.shape
    nz, ny, nx = C.shape
    size = nz * ny
    half = nx // 2
    shot = lax.axis_index("shot")
    s = lax.axis_index("slab")
    b = lax.axis_index("rep")
    c = lax.axis_index("sub")

    barrier = pltpu.get_barrier_semaphore()
    for d in range(1, nslab):
        pl.semaphore_signal(
            barrier, inc=1, device_id={"slab": lax.rem(s + d, nslab)}, device_id_type=MESH
        )
    for other in ({"shot": 1 - shot}, {"rep": 1 - b}, {"sub": 1 - c}):
        pl.semaphore_signal(barrier, inc=1, device_id=other, device_id_type=MESH)
    greeted = nslab + 2

    def rows_of(c_):
        return pl.ds(pl.multiple_of(c_ * cy, 8), cy)

    def lanes_of(h):
        return pl.ds(pl.multiple_of(h * half, 128), half)

    def u_at(t, c_, h):
        return U.at[:, pl.ds(t * cz, cz), rows_of(c_), lanes_of(h)]

    def u_full(t, c_):
        return U.at[:, pl.ds(t * cz, cz), rows_of(c_), :]

    def c_at(t, c_, h):
        return C.at[pl.ds(t * cz, cz), rows_of(c_), lanes_of(h)]

    def c_full(t, c_):
        return C.at[pl.ds(t * cz, cz), rows_of(c_), :]

    fetch = [
        pltpu.make_async_copy(src, dst, in_s.at[i])
        for i, (src, dst) in enumerate(
            [
                (now_in, U.at[0, pl.ds(s * cz, cz), rows_of(c), lanes_of(b)]),
                (prev_in, U.at[1, pl.ds(s * cz, cz), rows_of(c), lanes_of(b)]),
                (cour, c_full(s, c)),
                (seeds_in, seeds),
                (wav_in, wav),
                (sz_in, sz),
                (sy_in, sy),
                (sx_in, sx),
                (rz_in, rz),
                (ry_in, ry),
                (rx_in, rx),
            ]
        )
    ]
    for copy in fetch:
        copy.start()

    def rcopy(piece, ss, rs, device):
        return pltpu.make_async_remote_copy(
            src_ref=piece,
            dst_ref=piece,
            send_sem=ss,
            recv_sem=rs,
            device_id=device,
            device_id_type=MESH,
        )

    dists = []
    for d in range(nslab - 1, 0, -1):
        dists += [d, -d]

    def inside(t):
        return (t >= 0) & (t < nslab)

    def z_u(i, t, target):
        return rcopy(u_at(t, c, b), zu_s.at[i], zu_r.at[i], {"slab": target})

    def z_c(i, t, target):
        return rcopy(c_at(t, c, shot), zc_s.at[i], zc_r.at[i], {"slab": target})

    def x_u(i, t, h):
        return rcopy(u_at(t, c, h), xu_s.at[i], xu_r.at[i], {"rep": 1 - b})

    def y_c(i, t, h):
        return rcopy(c_at(t, c, h), yc_s.at[i], yc_r.at[i], {"shot": 1 - shot})

    def sub_u(i, t, c_):
        return rcopy(u_full(t, c_), su_s.at[i], su_r.at[i], {"sub": 1 - c})

    def sub_c(i, t, c_):
        return rcopy(c_full(t, c_), sc_s.at[i], sc_r.at[i], {"sub": 1 - c})

    for copy in fetch[:3]:
        copy.wait()
    pl.semaphore_wait(barrier, greeted)

    x_u(0, s, b).start()
    for i, d in enumerate(dists):

        @pl.when(inside(s + d))
        def _():
            z_u(i, s, s + d).start()
            z_c(i, s, s + d).start()

    sub_c(0, s, c).start()

    rowy = lax.broadcasted_iota(jnp.int32, (ny, size), 0)
    col = lax.broadcasted_iota(jnp.int32, (ny, size), 1)
    colz, coly = col // ny, col % ny

    @pl.loop(0, nz)
    def _(z):
        gap = jnp.where(
            rowy == coly, jnp.abs(z - colz), jnp.where(z == colz, jnp.abs(rowy - coly), 0)
        )
        A[pl.ds(pl.multiple_of(z * ny, 16), ny), :] = tap_of(gap).astype(jnp.bfloat16)

    gap = jnp.abs(
        lax.broadcasted_iota(jnp.int32, (nx, nx), 0) - lax.broadcasted_iota(jnp.int32, (nx, nx), 1)
    )
    taps = tap_of(gap).astype(jnp.bfloat16)
    B2[pl.ds(0, nx), :] = taps
    B2[pl.ds(nx, nx), :] = taps

    for copy in fetch[3:]:
        copy.wait()
    ycoord = lax.broadcasted_iota(jnp.int32, (ny, nx), 0)
    xcoord = lax.broadcasted_iota(jnp.int32, (ny, nx), 1)
    flat = ycoord * 19349663 + xcoord * 83492791

    @pl.loop(0, nz)
    def _(z):
        for r in range(2):
            h = flat + (seeds[r] * 668265263 + z * 73856093)
            h = jnp.bitwise_xor(h, jnp.right_shift(h, 15))
            h = h * 1274126177
            h = jnp.bitwise_xor(h, jnp.right_shift(h, 13))
            f = jnp.bitwise_and(h, 65535).astype(jnp.float32)
            K[r, z] = f * (0.8 / 65535.0) - 0.4

    nsrc = sx.shape[0]
    lane = lax.broadcasted_iota(jnp.int32, (1, nsrc), 1)
    place = jnp.zeros((1, nsrc), jnp.int32)
    column = jnp.zeros((nsrc, nx), jnp.int32)
    ksub = lax.broadcasted_iota(jnp.int32, (nsrc, nx), 0)
    for k in range(nsrc):
        place = jnp.where(lane == k, sz[k] * ny + sy[k], place)
        column = jnp.where(ksub == k, sx[k], column)
    hit_x = jnp.where(lax.broadcasted_iota(jnp.int32, (nsrc, nx), 1) == column, 1.0, 0.0)
    hit = lax.broadcasted_iota(jnp.int32, (size, nsrc), 0) == place
    for n in range(STEPS):
        amounts = jnp.zeros((1, nsrc), jnp.float32)
        for k in range(nsrc):
            amounts = jnp.where(lane == k, wav[n, k], amounts)
        rows = jnp.where(hit, amounts, 0.0)
        INJ[n] = jnp.dot(rows, hit_x, precision=HI, preferred_element_type=jnp.float32).reshape(
            nz, ny, nx
        )

    nrec = rz.shape[0]
    sub_j = lax.broadcasted_iota(jnp.int32, (nrec, 128), 0)
    jz = jnp.zeros((nrec, 128), jnp.int32)
    jy = jnp.zeros((nrec, 128), jnp.int32)
    jx = jnp.zeros((nrec, 128), jnp.int32)
    for j in range(nrec):
        jz = jnp.where(sub_j == j, rz[j], jz)
        jy = jnp.where(sub_j == j, ry[j], jy)
        jx = jnp.where(sub_j == j, rx[j], jx)
    lane_j = lax.broadcasted_iota(jnp.int32, (nrec, 128), 1)
    for q in range(size // 128):
        z, y = (q * 128 + lane_j) // ny, (q * 128 + lane_j) % ny
        dz, dy = jnp.abs(z - jz), jnp.abs(y - jy)
        here = jnp.where(dz + dy == 0, 1.0, 0.0).astype(jnp.bfloat16)
        gap = jnp.where(dy == 0, dz, jnp.where(dz == 0, dy, 0))
        near = tap_of(gap).astype(jnp.bfloat16)
        for part in range(2):
            G2[pl.ds(0, nrec), pl.ds(part * size + q * 128, 128)] = here
            G2[pl.ds(nrec, nrec), pl.ds(part * size + q * 128, 128)] = near
    for q in range(nx // 128):
        gap = jnp.abs(q * 128 + lane_j - jx)
        RX[0, :, pl.ds(q * 128, 128)] = jnp.where(gap == 0, 1.0, 0.0)
        RX[1, :, pl.ds(q * 128, 128)] = tap_of(gap) + jnp.where(gap == 0, TAPS[0], 0.0)
    for j in range(nrec):
        for r in range(2):
            RR[r, pl.ds(j, 1), :] = K[r, rz[j], pl.ds(ry[j], 1), :]
        RR[2, pl.ds(j, 1), :] = INJ[STEPS - 1, rz[j], pl.ds(ry[j], 1), :]

    x_u(0, s, 1 - b).wait_recv()
    sub_u(0, s, c).start()
    for i, d in enumerate(dists):

        @pl.when(inside(s - d))
        def _():
            z_u(i, s - d, s).wait_recv()
            x_u(i + 1, s - d, b).start()
            z_c(i, s - d, s).wait_recv()
            y_c(i + 1, s - d, shot).start()

    for i, d in enumerate(dists):

        @pl.when(inside(s - d))
        def _():
            y_c(i + 1, s - d, 1 - shot).wait_recv()
            sub_c(i + 1, s - d, c).start()
            x_u(i + 1, s - d, 1 - b).wait_recv()
            sub_u(i + 1, s - d, c).start()

    sub_c(0, s, 1 - c).wait_recv()
    sub_u(0, s, 1 - c).wait_recv()
    for i, d in enumerate(dists):

        @pl.when(inside(s - d))
        def _():
            sub_c(i + 1, s - d, 1 - c).wait_recv()
            sub_u(i + 1, s - d, 1 - c).wait_recv()

    x_u(0, s, b).wait_send()
    sub_c(0, s, c).wait_send()
    sub_u(0, s, c).wait_send()
    for i, d in enumerate(dists):

        @pl.when(inside(s + d))
        def _():
            z_u(i, s, s + d).wait_send()
            z_c(i, s, s + d).wait_send()

        @pl.when(inside(s - d))
        def _():
            x_u(i + 1, s - d, b).wait_send()
            y_c(i + 1, s - d, shot).wait_send()
            sub_c(i + 1, s - d, c).wait_send()
            sub_u(i + 1, s - d, c).wait_send()


def advance(
    rz_in,
    ry_in,
    U0,
    C,
    K,
    INJ,
    A,
    B2,
    G2,
    RX,
    RR,
    inc_out,
    wave_out,
    trace_out,
    U,
    W,
    HL,
    SP,
    INC,
    WAVE,
    TR,
    RC,
    rz,
    ry,
    in_s,
    out_s,
):
    cz, cy, pw = inc_out.shape
    nz, ny, nx = C.shape
    size = nz * ny
    nrec = rz.shape[0]
    s = lax.axis_index("slab")
    b = lax.axis_index("rep")
    c = lax.axis_index("sub")
    fetch = [
        pltpu.make_async_copy(src, dst, in_s.at[i])
        for i, (src, dst) in enumerate([(rz_in, rz), (ry_in, ry)])
    ]
    for copy in fetch:
        copy.start()

    slabs = nz // cz
    rows = cz * ny

    def split(buf, field, z, v):
        high = v.astype(jnp.bfloat16)
        HL[buf, 0, z, :, pl.ds(field * nx, nx)] = high
        HL[buf, 1, z, :, pl.ds(field * nx, nx)] = (v - high.astype(jnp.float32)).astype(
            jnp.bfloat16
        )

    def parts(buf, field, z0, count):
        xs = pl.ds(field * nx, nx)
        return [HL[buf, p, pl.ds(z0, count), :, xs].reshape(count * ny, nx) for p in range(2)]

    def lap_slab(buf, field, t):
        lo, hi = max(t - 1, 0), min(t + 2, slabs)
        a = A[pl.ds(t * rows, rows), pl.ds(lo * rows, (hi - lo) * rows)]
        lhs = jnp.concatenate([a, a] + parts(buf, field, t * cz, cz), axis=1)
        rhs = jnp.concatenate(parts(buf, field, lo * cz, (hi - lo) * cz) + [B2[...]], axis=0)
        return jnp.dot(lhs, rhs, preferred_element_type=jnp.float32)

    def at_receivers(buf, field, count):
        rhs = jnp.concatenate(parts(buf, field, 0, nz), axis=0)
        return jnp.dot(G2[pl.ds(0, count), :], rhs, preferred_element_type=jnp.float32)

    def pick(rows):
        return jnp.sum(rows, axis=1, keepdims=True)

    @pl.loop(0, nz, unroll=2)
    def _(z):
        split(0, 0, z, U0[0, z])
        SP[z] = C[z] * C[z] * (1.0 / SCALE)

    seen = {}
    for n in range(STEPS - 1):
        now, before = n % 2, 1 - n % 2
        wnow, wnext = (n + 1) % 2, n % 2
        buf, nbuf = n % 2, 1 - n % 2
        unow = U0 if n == 0 else U
        uold = U0 if n < 2 else U
        for t in range(slabs):
            laps = [lap_slab(buf, f, t) for f in range(3 if n > 0 else 1)]
            for i in range(cz):
                z = t * cz + i
                part = [v[i * ny : i * ny + ny] for v in laps]
                speed = SP[z]
                mid = unow[now, z]
                delta = speed * (part[0] + TAPS[0] * mid) + INJ[n, z]
                v = 2.0 * mid - uold[before, z] + delta
                U[before, z] = v
                split(nbuf, 0, z, v)
                for r in range(2):
                    v = K[r, z] * delta
                    if n > 0:
                        mid = W[wnow, r, z]
                        v = v + (speed * (part[1 + r] + TAPS[0] * mid) + 2.0 * mid)
                    if n > 1:
                        v = v - W[wnext, r, z]
                    W[wnext, r, z] = v
                    split(nbuf, 1 + r, z, v)
        if n > 0:
            for r in range(2):
                seen[n, r] = pick(at_receivers(buf, 1 + r, nrec) * RX[0])

    for copy in fetch:
        copy.wait()
    for j in range(nrec):
        RC[pl.ds(j, 1), :] = SP[rz[j], pl.ds(ry[j], 1), :]

    n = STEPS - 1
    now, before = n % 2, 1 - n % 2
    wnow, wnext = (n + 1) % 2, n % 2
    own_z = pl.ds(s * cz, cz)
    own_y = pl.ds(pl.multiple_of(c * cy, 16), cy)
    lanes = pl.ds(pl.multiple_of(b * pw, 128), pw)
    area = cz * cy

    def own(ref, *lead):
        return ref[(*lead, own_z, own_y, slice(None))].reshape(area, nx)

    first = pl.multiple_of(s * cz * ny + c * cy, 16)
    own_a = jnp.concatenate(
        [A[pl.ds(pl.multiple_of(first + z * ny, 16), cy), :] for z in range(cz)], axis=0
    )
    speed = own(SP)
    speed_j = pick(RC[...] * RX[0])

    def last(field, mid):
        high, low = parts(n % 2, field, 0, nz)
        xs = pl.ds(field * nx, nx)
        mine = [HL[n % 2, p, own_z, own_y, xs].reshape(area, nx) for p in range(2)]
        lhs = jnp.concatenate([jnp.concatenate([own_a, own_a], axis=1), G2[...]], axis=0)
        out = jnp.dot(
            lhs, jnp.concatenate([high, low], axis=0), preferred_element_type=jnp.float32
        )
        across = jnp.dot(
            jnp.concatenate(mine, axis=1), B2[...], preferred_element_type=jnp.float32
        )
        here = out[area : area + nrec]
        lap_j = pick(out[area + nrec :] * RX[0] + here * RX[1])
        return out[:area] + across + TAPS[0] * mid, pick(here * RX[0]), lap_j

    mid = own(U, now)
    lap, _, lap_j = last(0, mid)
    delta = speed * lap + own(INJ, n)
    INC[...] = (2.0 * mid - own(U, before) + delta).reshape(cz, cy, nx)
    outs = [pltpu.make_async_copy(INC.at[:, :, lanes], inc_out, out_s.at[0])]
    outs[0].start()
    delta_j = speed_j * lap_j + pick(RR[2] * RX[0])
    for r in range(2):
        mid = own(W, wnow, r)
        lap, here, lap_j = last(1 + r, mid)
        v = own(K, r) * delta + speed * lap + 2.0 * mid - own(W, wnext, r)
        WAVE[r] = v.reshape(cz, cy, nx)
        outs.append(pltpu.make_async_copy(WAVE.at[r], wave_out.at[r], out_s.at[1 + r]))
        outs[-1].start()
        seen[n, r] = here
        kick = pick(RR[r] * RX[0]) * delta_j
        seen[n + 1, r] = 2.0 * here - seen[n - 1, r] + speed_j * lap_j + kick
    lane = lax.broadcasted_iota(jnp.int32, (nrec, 128), 1)
    table = jnp.zeros((nrec, 128), jnp.float32)
    for n in range(STEPS):
        for r in range(2):
            table = jnp.where(lane == 2 * n + r, seen[n + 1, r], table)
    table = table.T
    for n in range(STEPS):
        TR[n] = table[2 * n : 2 * n + 2, :nrec]
    outs.append(pltpu.make_async_copy(TR, trace_out, out_s.at[3]))
    outs[-1].start()
    for copy in outs:
        copy.wait()


def whole(nslab, courant, prev, now, wavelet, sz, sy, sx, seeds, rz, ry, rx):
    cz, cy, pw = now.shape
    nx = courant.shape[2]
    nz, ny = nslab * cz, 2 * cy
    size = nz * ny
    nrec = rz.shape[0]
    nd = 2 * (nslab - 1)
    hbm = pl.BlockSpec(memory_space=pltpu.HBM)
    vmem = pl.BlockSpec(memory_space=pltpu.VMEM)
    f32, bf16 = jnp.float32, jnp.bfloat16
    dma = pltpu.SemaphoreType.DMA
    fixed = [
        pltpu.with_memory_space_constraint(a, pltpu.HBM)
        for a in (seeds, wavelet, sz, sy, sx, rz, ry, rx, courant, prev, now)
    ]
    held = pl.pallas_call(
        functools.partial(gather, nslab),
        out_shape=(
            pltpu.VMEM((2, nz, ny, nx), f32),
            pltpu.VMEM((nz, ny, nx), f32),
            pltpu.VMEM((2, nz, ny, nx), f32),
            pltpu.VMEM((STEPS, nz, ny, nx), f32),
            pltpu.VMEM((size, size), bf16),
            pltpu.VMEM((2 * nx, nx), bf16),
            pltpu.VMEM((2 * nrec, 2 * size), bf16),
            pltpu.VMEM((2, nrec, nx), f32),
            pltpu.VMEM((3, nrec, nx), f32),
        ),
        in_specs=[hbm] * 11,
        out_specs=(vmem,) * 9,
        scratch_shapes=[dma((nd,))] * 4
        + [dma((nd + 1,))] * 8
        + [pltpu.SMEM(a.shape, a.dtype) for a in (seeds, wavelet, sz, sy, sx, rz, ry, rx)]
        + [dma((11,))],
        compiler_params=pltpu.CompilerParams(
            collective_id=0, has_side_effects=True, vmem_limit_bytes=56 << 20
        ),
    )(*fixed)
    return pl.pallas_call(
        functools.partial(advance),
        out_shape=(
            jax.ShapeDtypeStruct((cz, cy, pw), f32),
            jax.ShapeDtypeStruct((2, cz, cy, nx), f32),
            jax.ShapeDtypeStruct((STEPS, 2, nrec), f32),
        ),
        in_specs=[hbm] * 2 + [vmem] * 9,
        out_specs=(hbm,) * 3,
        scratch_shapes=[
            pltpu.VMEM((2, nz, ny, nx), f32),
            pltpu.VMEM((2, 2, nz, ny, nx), f32),
            pltpu.VMEM((2, 2, nz, ny, 3 * nx), bf16),
            pltpu.VMEM((nz, ny, nx), f32),
            pltpu.VMEM((cz, cy, nx), f32),
            pltpu.VMEM((2, cz, cy, nx), f32),
            pltpu.VMEM((STEPS, 2, nrec), f32),
            pltpu.VMEM((nrec, nx), f32),
            pltpu.SMEM(rz.shape, rz.dtype),
            pltpu.SMEM(ry.shape, ry.dtype),
            dma((2,)),
            dma((4,)),
        ],
        compiler_params=pltpu.CompilerParams(vmem_limit_bytes=32 << 20),
    )(fixed[5], fixed[6], *held)


def solution(mesh):
    nslab = mesh.shape["slab"]
    reach = min(4, nslab - 1)
    win = min(nslab, 9)

    def shards(courant, prev, now, wavelet, sz, sy, sx, seeds, rz, ry, rx):
        cz, cy, pw = now.shape
        nx = courant.shape[2]
        split = 2 * pw == nx and pw % 128 == 0
        if split and nslab <= 4 and cy % 16 == 0:
            return whole(nslab, courant, prev, now, wavelet, sz, sy, sx, seeds, rz, ry, rx)
        if not split:
            prev = lax.all_gather(prev, "rep", axis=2, tiled=True)
            now = lax.all_gather(now, "rep", axis=2, tiled=True)
        width = now.shape[2]
        ny = 2 * cy
        zw = win * cz
        nd = 2 * reach
        nrec = rz.shape[0]
        tw = -(-nrec // 128) * 128
        group = 2 * nslab
        hbm = pl.BlockSpec(memory_space=pltpu.HBM)
        vmem = pl.BlockSpec(memory_space=pltpu.VMEM)
        f32 = jnp.float32
        dma = pltpu.SemaphoreType.DMA
        inc, wave, traces = pl.pallas_call(
            functools.partial(windowed, nslab, split, reach, win),
            out_shape=(
                pltpu.VMEM((cz, cy, width), f32),
                pltpu.VMEM((2, cz, cy, nx), f32),
                pltpu.VMEM((STEPS, 2, nrec), f32),
            ),
            in_specs=[hbm] * 11,
            out_specs=(vmem, vmem, vmem),
            scratch_shapes=[
                pltpu.VMEM((2, zw + 2 * cz, ny + 16, nx), f32),
                pltpu.VMEM((zw + 2 * cz, ny, nx), f32),
                pltpu.VMEM((2, 2, zw + 2 * cz, ny + 16, nx), f32),
                pltpu.VMEM((2, zw, ny, nx), f32),
                pltpu.VMEM((STEPS, zw, ny, nx), f32),
                pltpu.VMEM((3, zw, ny, nx), f32),
                pltpu.VMEM((3 * nx, nx), jnp.bfloat16),
                pltpu.VMEM((32, nx), f32),
                pltpu.VMEM((group, 8, tw), f32),
            ]
            + [dma((nd,))] * 4
            + [dma((nd + 1,))] * 8
            + [dma((group,))] * 2
            + [pltpu.SMEM(a.shape, a.dtype) for a in (wavelet, sz, sy, sx, seeds, rz, ry, rx)]
            + [dma((11,))],
            compiler_params=pltpu.CompilerParams(
                collective_id=0, has_side_effects=True, vmem_limit_bytes=60 << 20
            ),
        )(wavelet, sz, sy, sx, seeds, rz, ry, rx, courant, prev, now)
        if not split:
            pw0 = width // lax.axis_size("rep")
            inc = lax.dynamic_slice_in_dim(inc, lax.axis_index("rep") * pw0, pw0, 2)
        return inc, wave, traces

    return jax.shard_map(
        shards,
        mesh=mesh,
        in_specs=(
            P("slab", "sub", None),
            P(("shot", "slab"), "sub", "rep"),
            P(("shot", "slab"), "sub", "rep"),
            P(),
            P("shot"),
            P("shot"),
            P("shot"),
            P("rep"),
            P(),
            P(),
            P(),
        ),
        out_specs=(
            P(("shot", "slab"), "sub", "rep"),
            P("rep", ("shot", "slab"), "sub", None),
            P("shot", "rep", None),
        ),
        check_vma=False,
    )
```

```python
import functools
import jax
import jax.numpy as jnp
from jax import lax
from jax.experimental import pallas as pl
from jax.experimental.pallas import tpu as pltpu
from jax.sharding import PartitionSpec as P

STEPS = 4
COEF = (-205.0 / 72.0, 8.0 / 5.0, -1.0 / 5.0, 8.0 / 315.0, -1.0 / 560.0)
MESH = pl.DeviceIdType.MESH
HI = lax.Precision.HIGHEST


def windowed(
    nslab,
    split,
    reach,
    win,
    wav_in,
    sz_in,
    sy_in,
    sx_in,
    seeds_in,
    rz_in,
    ry_in,
    rx_in,
    cour,
    prev_in,
    now_in,
    inc_out,
    wave_out,
    trace_out,
    U,
    C,
    W,
    K,
    INJ,
    XP,
    BAND,
    ROWS,
    TB,
    zu_s,
    zu_r,
    zc_s,
    zc_r,
    xu_s,
    xu_r,
    yc_s,
    yc_r,
    su_s,
    su_r,
    sc_s,
    sc_r,
    t_s,
    t_r,
    wav,
    sz,
    sy,
    sx,
    seeds,
    rz,
    ry,
    rx,
    in_s,
):
    cz, cy, pw = now_in.shape
    nx = cour.shape[2]
    ny = 2 * cy
    zw = win * cz
    nrec = trace_out.shape[2]
    half = nx // 2
    shot = lax.axis_index("shot")
    s = lax.axis_index("slab")
    b = lax.axis_index("rep")
    c = lax.axis_index("sub")

    def base_of(t):
        return jnp.clip(t - reach, 0, nslab - win)

    base = base_of(s)

    barrier = pltpu.get_barrier_semaphore()
    others = []
    for d in range(1, 2 * nslab):
        other = lax.rem(s * 2 + c + d, 2 * nslab)
        others.append(other)
        pl.semaphore_signal(
            barrier,
            inc=1,
            device_id={"slab": lax.div(other, 2), "sub": lax.rem(other, 2)},
            device_id_type=MESH,
        )
    pl.semaphore_signal(barrier, inc=1, device_id={"shot": 1 - shot}, device_id_type=MESH)
    greeted = 2 * nslab
    if split:
        pl.semaphore_signal(barrier, inc=1, device_id={"rep": 1 - b}, device_id_type=MESH)
        greeted += 1

    def zpos(t, of):
        return cz + (t - of) * cz

    def ypos(c_):
        return pl.multiple_of(8 + c_ * cy, 8)

    def xpos(h, width):
        return pl.multiple_of(h * width, 128)

    own_z = zpos(s, base)
    xown = pl.ds(xpos(b, pw), pw) if split else pl.ds(0, pw)
    fetch = [
        pltpu.make_async_copy(src, dst, in_s.at[i])
        for i, (src, dst) in enumerate(
            [
                (now_in, U.at[0, pl.ds(own_z, cz), pl.ds(ypos(c), cy), xown]),
                (prev_in, U.at[1, pl.ds(own_z, cz), pl.ds(ypos(c), cy), xown]),
                (cour, C.at[pl.ds(own_z, cz), pl.ds(pl.multiple_of(c * cy, 8), cy), :]),
                (seeds_in, seeds),
                (wav_in, wav),
                (sz_in, sz),
                (sy_in, sy),
                (sx_in, sx),
                (rz_in, rz),
                (ry_in, ry),
                (rx_in, rx),
            ]
        )
    ]
    for copy in fetch:
        copy.start()

    def u_piece(t, of, h):
        xs = pl.ds(xpos(h, pw), pw) if split else pl.ds(0, pw)
        return U.at[:, pl.ds(zpos(t, of), cz), pl.ds(ypos(c), cy), xs]

    def near(rows, c_):
        return pl.multiple_of((1 - c_) * (cy - rows), 8)

    def u_near(t, d, c_):
        rows = max(8, min(cy, -(-(16 - 4 * abs(d)) // 8) * 8))
        fields = pl.ds(0, 1 if abs(d) >= 3 else 2)
        return U.at[fields, pl.ds(zpos(t, base), cz), pl.ds(ypos(c_) + near(rows, c_), rows), :]

    def c_near(t, d, c_):
        rows = min(cy, -(-(12 - 4 * abs(d)) // 8) * 8)
        start = pl.multiple_of(c_ * cy, 8) + near(rows, c_)
        return C.at[pl.ds(zpos(t, base), cz), pl.ds(start, rows), :]

    def c_rows(t, of, c_, h):
        rows = pl.ds(pl.multiple_of(c_ * cy, 8), cy)
        xs = pl.ds(0, nx) if h is None else pl.ds(xpos(h, half), half)
        return C.at[pl.ds(zpos(t, of), cz), rows, xs]

    def rcopy(src, dst, ss, rs, device):
        return pltpu.make_async_remote_copy(
            src_ref=src, dst_ref=dst, send_sem=ss, recv_sem=rs, device_id=device, device_id_type=MESH
        )

    dists = []
    for d in range(reach, 0, -1):
        dists += [d, -d]

    for copy in fetch[:3]:
        copy.wait()
    pl.semaphore_wait(barrier, greeted)

    def z_copies(i, d):
        t = s + d
        of = base_of(t)
        return (
            rcopy(u_piece(s, base, b), u_piece(s, of, b), zu_s.at[i], zu_r.at[i], {"slab": t}),
            rcopy(
                c_rows(s, base, c, shot),
                c_rows(s, of, c, shot),
                zc_s.at[i],
                zc_r.at[i],
                {"slab": t},
            ),
        )

    def inside(t):
        return (t >= 0) & (t < nslab)

    def x_copy(i, t, h):
        return rcopy(u_piece(t, base, h), u_piece(t, base, h), xu_s.at[i], xu_r.at[i], {"rep": 1 - b})

    def y_copy(i, t, h):
        return rcopy(
            c_rows(t, base, c, h), c_rows(t, base, c, h), yc_s.at[i], yc_r.at[i], {"shot": 1 - shot}
        )

    def sub_u(i, t, d, mine):
        row = u_near(t, d, c if mine else 1 - c)
        return rcopy(row, row, su_s.at[i], su_r.at[i], {"sub": 1 - c})

    def sub_c(i, t, d, mine):
        row = c_near(t, d, c if mine else 1 - c)
        return rcopy(row, row, sc_s.at[i], sc_r.at[i], {"sub": 1 - c})

    if split:
        x_copy(0, s, b).start()
    for i, d in enumerate(dists):

        @pl.when(inside(s + d))
        def _():
            u_copy, c_copy = z_copies(i, d)
            u_copy.start()
            c_copy.start()

    sub_c(0, s, 0, True).start()

    wp = W.shape[-2]
    for buf in range(2):
        U[buf, pl.ds(0, cz)] = jnp.zeros((cz, wp, nx), jnp.float32)
        U[buf, pl.ds(cz + zw, cz)] = jnp.zeros((cz, wp, nx), jnp.float32)
        U[buf, pl.ds(cz, zw), pl.ds(0, 8), :] = jnp.zeros((zw, 8, nx), jnp.float32)
        U[buf, pl.ds(cz, zw), pl.ds(8 + ny, 8), :] = jnp.zeros((zw, 8, nx), jnp.float32)
        for r in range(2):
            W[buf, r, pl.ds(0, cz)] = jnp.zeros((cz, wp, nx), jnp.float32)
            W[buf, r, pl.ds(cz + zw, cz)] = jnp.zeros((cz, wp, nx), jnp.float32)
            W[buf, r, pl.ds(cz, zw), pl.ds(0, 8), :] = jnp.zeros((zw, 8, nx), jnp.float32)
            W[buf, r, pl.ds(cz, zw), pl.ds(8 + ny, 8), :] = jnp.zeros((zw, 8, nx), jnp.float32)

    gap = jnp.abs(
        lax.broadcasted_iota(jnp.int32, (nx, nx), 0) - lax.broadcasted_iota(jnp.int32, (nx, nx), 1)
    )
    band = jnp.zeros((nx, nx), jnp.float32)
    for k in range(1, 5):
        band = jnp.where(gap == k, COEF[k], band)
    high = band.astype(jnp.bfloat16)
    BAND[pl.ds(0, nx), :] = high
    BAND[pl.ds(nx, nx), :] = high
    BAND[pl.ds(2 * nx, nx), :] = (band - high.astype(jnp.float32)).astype(jnp.bfloat16)

    for copy in fetch[3:]:
        copy.wait()
    ycoord = lax.broadcasted_iota(jnp.int32, (ny, nx), 0)
    xcoord = lax.broadcasted_iota(jnp.int32, (ny, nx), 1)
    flat = ycoord * 19349663 + xcoord * 83492791

    @pl.loop(0, zw)
    def _(z):
        for r in range(2):
            h = flat + (seeds[r] * 668265263 + (base * cz + z) * 73856093)
            h = jnp.bitwise_xor(h, jnp.right_shift(h, 15))
            h = h * 1274126177
            h = jnp.bitwise_xor(h, jnp.right_shift(h, 13))
            f = jnp.bitwise_and(h, 65535).astype(jnp.float32)
            K[r, z] = f * (0.8 / 65535.0) - 0.4

    nsrc = sx.shape[0]
    lane = lax.broadcasted_iota(jnp.int32, (1, nsrc), 1)
    place = jnp.zeros((1, nsrc), jnp.int32)
    column = jnp.zeros((nsrc, nx), jnp.int32)
    ksub = lax.broadcasted_iota(jnp.int32, (nsrc, nx), 0)
    for k in range(nsrc):
        place = jnp.where(lane == k, (sz[k] - base * cz) * ny + sy[k], place)
        column = jnp.where(ksub == k, sx[k], column)
    hit_x = jnp.where(lax.broadcasted_iota(jnp.int32, (nsrc, nx), 1) == column, 1.0, 0.0)
    row_id = lax.broadcasted_iota(jnp.int32, (zw * ny, nsrc), 0)
    hit = row_id == place
    for n in range(STEPS):
        amounts = jnp.zeros((1, nsrc), jnp.float32)
        for k in range(nsrc):
            amounts = jnp.where(lane == k, wav[n, k], amounts)
        rows = jnp.where(hit, amounts, 0.0)
        INJ[n] = jnp.dot(rows, hit_x, precision=HI, preferred_element_type=jnp.float32).reshape(
            zw, ny, nx
        )

    def hand_over(i, d):
        @pl.when(inside(s - d))
        def _():
            t = s - d
            y_copy(i + 1, t, 1 - shot).wait_recv()
            if abs(d) < 3:
                sub_c(i + 1, t, d, True).start()
            if split:
                x_copy(i + 1, t, 1 - b).wait_recv()
            if abs(d) < 4:
                sub_u(i + 1, t, d, True).start()

    if split:
        x_copy(0, s, 1 - b).wait_recv()
    sub_u(0, s, 0, True).start()
    for i, d in enumerate(dists):

        @pl.when(inside(s - d))
        def _():
            t = s - d
            mine = u_piece(t, base, b)
            rcopy(mine, mine, zu_s.at[i], zu_r.at[i], {"slab": s}).wait_recv()
            if split:
                x_copy(i + 1, t, b).start()
            mine = c_rows(t, base, c, shot)
            rcopy(mine, mine, zc_s.at[i], zc_r.at[i], {"slab": s}).wait_recv()
            y_copy(i + 1, t, shot).start()

    for i, d in enumerate(dists):
        hand_over(i, d)

    sub_c(0, s, 0, False).wait_recv()
    sub_u(0, s, 0, False).wait_recv()
    for i, d in enumerate(dists):

        @pl.when(inside(s - d))
        def _():
            if abs(d) < 3:
                sub_c(i + 1, s - d, d, False).wait_recv()
            if abs(d) < 4:
                sub_u(i + 1, s - d, d, False).wait_recv()

    if split:
        x_copy(0, s, b).wait_send()
    sub_c(0, s, 0, True).wait_send()
    sub_u(0, s, 0, True).wait_send()
    for i, d in enumerate(dists):

        @pl.when(inside(s + d))
        def _():
            u_copy, c_copy = z_copies(i, d)
            u_copy.wait_send()
            c_copy.wait_send()

        @pl.when(inside(s - d))
        def _():
            t = s - d
            if split:
                x_copy(i + 1, t, b).wait_send()
            y_copy(i + 1, t, shot).wait_send()
            if abs(d) < 3:
                sub_c(i + 1, t, d, True).wait_send()
            if abs(d) < 4:
                sub_u(i + 1, t, d, True).wait_send()

    core = (s - base) * cz
    j0 = (s * 2 + c) * 4

    def step(n, y0, rows):
        now, before = n % 2, 1 - n % 2
        left = STEPS - 1 - n
        nz = min(zw, cz + 8 * left)
        z0 = jnp.clip(core - 4 * left, 0, zw - nz)
        wnow, wnext = (n + 1) % 2, n % 2
        ys = pl.ds(8 + y0, rows)
        yc = pl.ds(y0, rows)

        def across(ref):
            v = ref[pl.ds(cz + z0, nz), ys, :].reshape(nz * rows, nx)
            high = v.astype(jnp.bfloat16)
            low = (v - high.astype(jnp.float32)).astype(jnp.bfloat16)
            both = jnp.concatenate([high, low, high], axis=1)
            out = jnp.dot(both, BAND[...], preferred_element_type=jnp.float32)
            return out.reshape(nz, rows, nx)

        XP[0, pl.ds(0, nz), pl.ds(0, rows), :] = across(U.at[now])
        if n > 0:
            for r in range(2):
                XP[1 + r, pl.ds(0, nz), pl.ds(0, rows), :] = across(W.at[wnow, r])

        @pl.loop(0, nz, unroll=4)
        def _(i):
            z = z0 + i
            p = z + cz
            speed = C[p, yc, :]
            speed = speed * speed

            def lap(ref, mid, part):
                acc = part + (3.0 * COEF[0]) * mid
                for k in range(1, 5):
                    acc = acc + COEF[k] * (
                        (ref[p + k, ys, :] + ref[p - k, ys, :])
                        + (ref[p, pl.ds(8 + y0 + k, rows), :] + ref[p, pl.ds(8 + y0 - k, rows), :])
                    )
                return acc

            mid = U[now, p, ys, :]
            delta = speed * lap(U.at[now], mid, XP[0, i, pl.ds(0, rows), :]) + INJ[n, z, yc, :]
            U[before, p, ys, :] = 2.0 * mid - U[before, p, ys, :] + delta
            for r in range(2):
                term = K[r, z, yc, :] * delta
                if n > 0:
                    mid = W[wnow, r, p, ys, :]
                    term = term + speed * lap(W.at[wnow, r], mid, XP[1 + r, i, pl.ds(0, rows), :])
                    term = term + 2.0 * mid
                if n > 1:
                    term = term - W[wnext, r, p, ys, :]
                W[wnext, r, p, ys, :] = term

        for i in range(4):
            zj = rz[j0 + i] - base * cz + cz
            yj = ry[j0 + i] + 8
            for r in range(2):
                ROWS[pl.ds(i * 8 + n * 2 + r, 1), :] = W[wnext, r, zj, pl.ds(yj, 1), :]

    step(0, 0, ny)
    for side in range(2):

        @pl.when(c == side)
        def _():
            for n in range(1, STEPS):
                rows = min(ny, cy + 8 * -(-(STEPS - 1 - n) // 2))
                step(n, side * (ny - rows), rows)

    tw = TB.shape[2]
    lane_x = lax.broadcasted_iota(jnp.int32, (8, nx), 1)
    lane_j = lax.broadcasted_iota(jnp.int32, (8, tw), 1)
    tile = jnp.zeros((8, tw), jnp.float32)
    for i in range(4):
        picked = jnp.where(lane_x == rx[j0 + i], ROWS[pl.ds(i * 8, 8), :], 0.0)
        picked = jnp.sum(picked, axis=1, keepdims=True)
        tile = jnp.where(lane_j == j0 + i, picked, tile)
    me = s * 2 + c
    TB[me] = tile

    def t_copy(d, src, target):
        return rcopy(
            TB.at[src],
            TB.at[src],
            t_s.at[d],
            t_r.at[d],
            {"slab": lax.div(target, 2), "sub": lax.rem(target, 2)},
        )

    for d in range(1, 2 * nslab):
        t_copy(d, me, others[d - 1]).start()
    last = (STEPS - 1) % 2
    wave_out[...] = W[last, :, pl.ds(cz + core, cz), pl.ds(ypos(c), cy), :]
    if split:
        inc_out[...] = U[STEPS % 2, pl.ds(cz + core, cz), pl.ds(ypos(c), cy), xown]
    else:
        inc_out[...] = U[STEPS % 2, pl.ds(cz + core, cz), pl.ds(ypos(c), cy), :]

    for d in range(1, 2 * nslab):
        source = lax.rem(me + 2 * nslab - d, 2 * nslab)
        t_copy(d, source, others[d - 1]).wait_recv()
        tile = tile + TB[source]
    for d in range(1, 2 * nslab):
        t_copy(d, me, others[d - 1]).wait_send()
    for n in range(STEPS):
        trace_out[n] = tile[2 * n : 2 * n + 2, :nrec]


SCALE = 5040.0 / 4096.0
TAPS = tuple(v / 4096.0 for v in (-43050.0, 8064.0, -1008.0, 128.0, -9.0))


def tap_of(gap):
    out = jnp.where(gap == 1, TAPS[1], 0.0)
    for k in range(2, 5):
        out = jnp.where(gap == k, TAPS[k], out)
    return out


def gather(
    nslab,
    seeds_in,
    wav_in,
    sz_in,
    sy_in,
    sx_in,
    rz_in,
    ry_in,
    rx_in,
    cour,
    prev_in,
    now_in,
    U,
    C,
    K,
    INJ,
    A,
    B2,
    G2,
    RX,
    RR,
    zu_s,
    zu_r,
    zc_s,
    zc_r,
    xu_s,
    xu_r,
    yc_s,
    yc_r,
    su_s,
    su_r,
    sc_s,
    sc_r,
    seeds,
    wav,
    sz,
    sy,
    sx,
    rz,
    ry,
    rx,
    in_s,
):
    cz, cy, pw = now_in.shape
    nz, ny, nx = C.shape
    size = nz * ny
    half = nx // 2
    shot = lax.axis_index("shot")
    s = lax.axis_index("slab")
    b = lax.axis_index("rep")
    c = lax.axis_index("sub")

    barrier = pltpu.get_barrier_semaphore()
    for d in range(1, nslab):
        pl.semaphore_signal(
            barrier, inc=1, device_id={"slab": lax.rem(s + d, nslab)}, device_id_type=MESH
        )
    for other in ({"shot": 1 - shot}, {"rep": 1 - b}, {"sub": 1 - c}):
        pl.semaphore_signal(barrier, inc=1, device_id=other, device_id_type=MESH)
    greeted = nslab + 2

    def rows_of(c_):
        return pl.ds(pl.multiple_of(c_ * cy, 8), cy)

    def lanes_of(h):
        return pl.ds(pl.multiple_of(h * half, 128), half)

    def u_at(t, c_, h):
        return U.at[:, pl.ds(t * cz, cz), rows_of(c_), lanes_of(h)]

    def u_full(t, c_):
        return U.at[:, pl.ds(t * cz, cz), rows_of(c_), :]

    def c_at(t, c_, h):
        return C.at[pl.ds(t * cz, cz), rows_of(c_), lanes_of(h)]

    def c_full(t, c_):
        return C.at[pl.ds(t * cz, cz), rows_of(c_), :]

    fetch = [
        pltpu.make_async_copy(src, dst, in_s.at[i])
        for i, (src, dst) in enumerate(
            [
                (now_in, U.at[0, pl.ds(s * cz, cz), rows_of(c), lanes_of(b)]),
                (prev_in, U.at[1, pl.ds(s * cz, cz), rows_of(c), lanes_of(b)]),
                (cour, c_full(s, c)),
                (seeds_in, seeds),
                (wav_in, wav),
                (sz_in, sz),
                (sy_in, sy),
                (sx_in, sx),
                (rz_in, rz),
                (ry_in, ry),
                (rx_in, rx),
            ]
        )
    ]
    for copy in fetch:
        copy.start()

    def rcopy(piece, ss, rs, device):
        return pltpu.make_async_remote_copy(
            src_ref=piece,
            dst_ref=piece,
            send_sem=ss,
            recv_sem=rs,
            device_id=device,
            device_id_type=MESH,
        )

    dists = []
    for d in range(nslab - 1, 0, -1):
        dists += [d, -d]

    def inside(t):
        return (t >= 0) & (t < nslab)

    def z_u(i, t, target):
        return rcopy(u_at(t, c, b), zu_s.at[i], zu_r.at[i], {"slab": target})

    def z_c(i, t, target):
        return rcopy(c_at(t, c, shot), zc_s.at[i], zc_r.at[i], {"slab": target})

    def x_u(i, t, h):
        return rcopy(u_at(t, c, h), xu_s.at[i], xu_r.at[i], {"rep": 1 - b})

    def y_c(i, t, h):
        return rcopy(c_at(t, c, h), yc_s.at[i], yc_r.at[i], {"shot": 1 - shot})

    def sub_u(i, t, c_):
        return rcopy(u_full(t, c_), su_s.at[i], su_r.at[i], {"sub": 1 - c})

    def sub_c(i, t, c_):
        return rcopy(c_full(t, c_), sc_s.at[i], sc_r.at[i], {"sub": 1 - c})

    for copy in fetch[:3]:
        copy.wait()
    pl.semaphore_wait(barrier, greeted)

    x_u(0, s, b).start()
    for i, d in enumerate(dists):

        @pl.when(inside(s + d))
        def _():
            z_u(i, s, s + d).start()
            z_c(i, s, s + d).start()

    sub_c(0, s, c).start()

    rowy = lax.broadcasted_iota(jnp.int32, (ny, size), 0)
    col = lax.broadcasted_iota(jnp.int32, (ny, size), 1)
    colz, coly = col // ny, col % ny

    @pl.loop(0, nz)
    def _(z):
        gap = jnp.where(
            rowy == coly, jnp.abs(z - colz), jnp.where(z == colz, jnp.abs(rowy - coly), 0)
        )
        A[pl.ds(pl.multiple_of(z * ny, 16), ny), :] = tap_of(gap).astype(jnp.bfloat16)

    gap = jnp.abs(
        lax.broadcasted_iota(jnp.int32, (nx, nx), 0) - lax.broadcasted_iota(jnp.int32, (nx, nx), 1)
    )
    taps = tap_of(gap).astype(jnp.bfloat16)
    B2[pl.ds(0, nx), :] = taps
    B2[pl.ds(nx, nx), :] = taps

    for copy in fetch[3:]:
        copy.wait()
    ycoord = lax.broadcasted_iota(jnp.int32, (ny, nx), 0)
    xcoord = lax.broadcasted_iota(jnp.int32, (ny, nx), 1)
    flat = ycoord * 19349663 + xcoord * 83492791

    @pl.loop(0, nz)
    def _(z):
        for r in range(2):
            h = flat + (seeds[r] * 668265263 + z * 73856093)
            h = jnp.bitwise_xor(h, jnp.right_shift(h, 15))
            h = h * 1274126177
            h = jnp.bitwise_xor(h, jnp.right_shift(h, 13))
            f = jnp.bitwise_and(h, 65535).astype(jnp.float32)
            K[r, z] = f * (0.8 / 65535.0) - 0.4

    nsrc = sx.shape[0]
    lane = lax.broadcasted_iota(jnp.int32, (1, nsrc), 1)
    place = jnp.zeros((1, nsrc), jnp.int32)
    column = jnp.zeros((nsrc, nx), jnp.int32)
    ksub = lax.broadcasted_iota(jnp.int32, (nsrc, nx), 0)
    for k in range(nsrc):
        place = jnp.where(lane == k, sz[k] * ny + sy[k], place)
        column = jnp.where(ksub == k, sx[k], column)
    hit_x = jnp.where(lax.broadcasted_iota(jnp.int32, (nsrc, nx), 1) == column, 1.0, 0.0)
    hit = lax.broadcasted_iota(jnp.int32, (size, nsrc), 0) == place
    for n in range(STEPS):
        amounts = jnp.zeros((1, nsrc), jnp.float32)
        for k in range(nsrc):
            amounts = jnp.where(lane == k, wav[n, k], amounts)
        rows = jnp.where(hit, amounts, 0.0)
        INJ[n] = jnp.dot(rows, hit_x, precision=HI, preferred_element_type=jnp.float32).reshape(
            nz, ny, nx
        )

    nrec = rz.shape[0]
    sub_j = lax.broadcasted_iota(jnp.int32, (nrec, 128), 0)
    jz = jnp.zeros((nrec, 128), jnp.int32)
    jy = jnp.zeros((nrec, 128), jnp.int32)
    jx = jnp.zeros((nrec, 128), jnp.int32)
    for j in range(nrec):
        jz = jnp.where(sub_j == j, rz[j], jz)
        jy = jnp.where(sub_j == j, ry[j], jy)
        jx = jnp.where(sub_j == j, rx[j], jx)
    lane_j = lax.broadcasted_iota(jnp.int32, (nrec, 128), 1)
    for q in range(size // 128):
        z, y = (q * 128 + lane_j) // ny, (q * 128 + lane_j) % ny
        dz, dy = jnp.abs(z - jz), jnp.abs(y - jy)
        here = jnp.where(dz + dy == 0, 1.0, 0.0).astype(jnp.bfloat16)
        gap = jnp.where(dy == 0, dz, jnp.where(dz == 0, dy, 0))
        near = tap_of(gap).astype(jnp.bfloat16)
        for part in range(2):
            G2[pl.ds(0, nrec), pl.ds(part * size + q * 128, 128)] = here
            G2[pl.ds(nrec, nrec), pl.ds(part * size + q * 128, 128)] = near
    for q in range(nx // 128):
        gap = jnp.abs(q * 128 + lane_j - jx)
        RX[0, :, pl.ds(q * 128, 128)] = jnp.where(gap == 0, 1.0, 0.0)
        RX[1, :, pl.ds(q * 128, 128)] = tap_of(gap) + jnp.where(gap == 0, TAPS[0], 0.0)
    for j in range(nrec):
        for r in range(2):
            RR[r, pl.ds(j, 1), :] = K[r, rz[j], pl.ds(ry[j], 1), :]
        RR[2, pl.ds(j, 1), :] = INJ[STEPS - 1, rz[j], pl.ds(ry[j], 1), :]

    def take(d):
        i = dists.index(d)
        z_u(i, s - d, s).wait_recv()
        x_u(i + 1, s - d, b).start()
        z_c(i, s - d, s).wait_recv()
        y_c(i + 1, s - d, shot).start()

    def hand_over(d):
        i = dists.index(d)
        y_c(i + 1, s - d, 1 - shot).wait_recv()
        sub_c(i + 1, s - d, c).start()
        x_u(i + 1, s - d, 1 - b).wait_recv()
        sub_u(i + 1, s - d, c).start()

    x_u(0, s, 1 - b).wait_recv()
    sub_u(0, s, c).start()
    for t in range(nslab):

        @pl.when(s == t)
        def _():
            near = sorted((t - o for o in range(nslab) if o != t), key=abs)
            if 0 < t < nslab - 1:
                inner = -1 if 2 * t < nslab else 1
                near = [d for d in near if d != inner][::-1] + [inner]
            else:
                near = near[:1] + near[1:][::-1]
            for d in near:
                take(d)
            for d in near:
                hand_over(d)

    sub_c(0, s, 1 - c).wait_recv()
    sub_u(0, s, 1 - c).wait_recv()
    for i, d in enumerate(dists):

        @pl.when(inside(s - d))
        def _():
            sub_c(i + 1, s - d, 1 - c).wait_recv()
            sub_u(i + 1, s - d, 1 - c).wait_recv()

    x_u(0, s, b).wait_send()
    sub_c(0, s, c).wait_send()
    sub_u(0, s, c).wait_send()
    for i, d in enumerate(dists):

        @pl.when(inside(s + d))
        def _():
            z_u(i, s, s + d).wait_send()
            z_c(i, s, s + d).wait_send()

        @pl.when(inside(s - d))
        def _():
            x_u(i + 1, s - d, b).wait_send()
            y_c(i + 1, s - d, shot).wait_send()
            sub_c(i + 1, s - d, c).wait_send()
            sub_u(i + 1, s - d, c).wait_send()


def advance(
    rz_in,
    ry_in,
    U0,
    C,
    K,
    INJ,
    A,
    B2,
    G2,
    RX,
    RR,
    inc_out,
    wave_out,
    trace_out,
    U,
    W,
    HL,
    SP,
    INC,
    WAVE,
    TR,
    RC,
    rz,
    ry,
    in_s,
    out_s,
):
    cz, cy, pw = inc_out.shape
    nz, ny, nx = C.shape
    size = nz * ny
    nrec = rz.shape[0]
    s = lax.axis_index("slab")
    b = lax.axis_index("rep")
    c = lax.axis_index("sub")
    fetch = [
        pltpu.make_async_copy(src, dst, in_s.at[i])
        for i, (src, dst) in enumerate([(rz_in, rz), (ry_in, ry)])
    ]
    for copy in fetch:
        copy.start()

    slabs = nz // cz
    rows = cz * ny

    def split(buf, field, z, v):
        high = v.astype(jnp.bfloat16)
        HL[buf, 0, z, :, pl.ds(field * nx, nx)] = high
        HL[buf, 1, z, :, pl.ds(field * nx, nx)] = (v - high.astype(jnp.float32)).astype(
            jnp.bfloat16
        )

    def parts(buf, field, z0, count):
        xs = pl.ds(field * nx, nx)
        return [HL[buf, p, pl.ds(z0, count), :, xs].reshape(count * ny, nx) for p in range(2)]

    def lap_slab(buf, field, t):
        lo, hi = max(t - 1, 0), min(t + 2, slabs)
        a = A[pl.ds(t * rows, rows), pl.ds(lo * rows, (hi - lo) * rows)]
        lhs = jnp.concatenate([a, a] + parts(buf, field, t * cz, cz), axis=1)
        rhs = jnp.concatenate(parts(buf, field, lo * cz, (hi - lo) * cz) + [B2[...]], axis=0)
        return jnp.dot(lhs, rhs, preferred_element_type=jnp.float32)

    def at_receivers(buf, field, count):
        rhs = jnp.concatenate(parts(buf, field, 0, nz), axis=0)
        return jnp.dot(G2[pl.ds(0, count), :], rhs, preferred_element_type=jnp.float32)

    def pick(rows):
        return jnp.sum(rows, axis=1, keepdims=True)

    for z in range(nz):
        split(0, 0, z, U0[0, z])
        SP[z] = C[z] * C[z] * (1.0 / SCALE)

    seen = {}
    for n in range(STEPS - 1):
        now, before = n % 2, 1 - n % 2
        wnow, wnext = (n + 1) % 2, n % 2
        buf, nbuf = n % 2, 1 - n % 2
        unow = U0 if n == 0 else U
        uold = U0 if n < 2 else U
        for t in range(slabs):
            laps = [lap_slab(buf, f, t) for f in range(3 if n > 0 else 1)]
            for i in range(cz):
                z = t * cz + i
                part = [v[i * ny : i * ny + ny] for v in laps]
                speed = SP[z]
                mid = unow[now, z]
                delta = speed * (part[0] + TAPS[0] * mid) + INJ[n, z]
                v = 2.0 * mid - uold[before, z] + delta
                U[before, z] = v
                split(nbuf, 0, z, v)
                for r in range(2):
                    v = K[r, z] * delta
                    if n > 0:
                        mid = W[wnow, r, z]
                        v = v + (speed * (part[1 + r] + TAPS[0] * mid) + 2.0 * mid)
                    if n > 1:
                        v = v - W[wnext, r, z]
                    W[wnext, r, z] = v
                    split(nbuf, 1 + r, z, v)
        if n > 0:
            for r in range(2):
                seen[n, r] = pick(at_receivers(buf, 1 + r, nrec) * RX[0])

    for copy in fetch:
        copy.wait()
    for j in range(nrec):
        RC[pl.ds(j, 1), :] = SP[rz[j], pl.ds(ry[j], 1), :]

    n = STEPS - 1
    now, before = n % 2, 1 - n % 2
    wnow, wnext = (n + 1) % 2, n % 2
    own_z = pl.ds(s * cz, cz)
    own_y = pl.ds(pl.multiple_of(c * cy, 16), cy)
    lanes = pl.ds(pl.multiple_of(b * pw, 128), pw)
    area = cz * cy

    def own(ref, *lead):
        return ref[(*lead, own_z, own_y, slice(None))].reshape(area, nx)

    first = pl.multiple_of(s * cz * ny + c * cy, 16)
    own_a = jnp.concatenate(
        [A[pl.ds(pl.multiple_of(first + z * ny, 16), cy), :] for z in range(cz)], axis=0
    )
    speed = own(SP)
    speed_j = pick(RC[...] * RX[0])

    def last(field, mid):
        high, low = parts(n % 2, field, 0, nz)
        xs = pl.ds(field * nx, nx)
        mine = [HL[n % 2, p, own_z, own_y, xs].reshape(area, nx) for p in range(2)]
        lhs = jnp.concatenate([jnp.concatenate([own_a, own_a], axis=1), G2[...]], axis=0)
        out = jnp.dot(
            lhs, jnp.concatenate([high, low], axis=0), preferred_element_type=jnp.float32
        )
        across = jnp.dot(
            jnp.concatenate(mine, axis=1), B2[...], preferred_element_type=jnp.float32
        )
        here = out[area : area + nrec]
        lap_j = pick(out[area + nrec :] * RX[0] + here * RX[1])
        return out[:area] + across + TAPS[0] * mid, pick(here * RX[0]), lap_j

    mid = own(U, now)
    lap, _, lap_j = last(0, mid)
    delta = speed * lap + own(INJ, n)
    INC[...] = (2.0 * mid - own(U, before) + delta).reshape(cz, cy, nx)
    outs = [pltpu.make_async_copy(INC.at[:, :, lanes], inc_out, out_s.at[0])]
    outs[0].start()
    delta_j = speed_j * lap_j + pick(RR[2] * RX[0])
    for r in range(2):
        mid = own(W, wnow, r)
        lap, here, lap_j = last(1 + r, mid)
        v = own(K, r) * delta + speed * lap + 2.0 * mid - own(W, wnext, r)
        WAVE[r] = v.reshape(cz, cy, nx)
        outs.append(pltpu.make_async_copy(WAVE.at[r], wave_out.at[r], out_s.at[1 + r]))
        outs[-1].start()
        seen[n, r] = here
        kick = pick(RR[r] * RX[0]) * delta_j
        seen[n + 1, r] = 2.0 * here - seen[n - 1, r] + speed_j * lap_j + kick
    lane = lax.broadcasted_iota(jnp.int32, (nrec, 128), 1)
    table = jnp.zeros((nrec, 128), jnp.float32)
    for n in range(STEPS):
        for r in range(2):
            table = jnp.where(lane == 2 * n + r, seen[n + 1, r], table)
    table = table.T
    for n in range(STEPS):
        TR[n] = table[2 * n : 2 * n + 2, :nrec]
    outs.append(pltpu.make_async_copy(TR, trace_out, out_s.at[3]))
    outs[-1].start()
    for copy in outs:
        copy.wait()


def whole(nslab, courant, prev, now, wavelet, sz, sy, sx, seeds, rz, ry, rx):
    cz, cy, pw = now.shape
    nx = courant.shape[2]
    nz, ny = nslab * cz, 2 * cy
    size = nz * ny
    nrec = rz.shape[0]
    nd = 2 * (nslab - 1)
    hbm = pl.BlockSpec(memory_space=pltpu.HBM)
    vmem = pl.BlockSpec(memory_space=pltpu.VMEM)
    f32, bf16 = jnp.float32, jnp.bfloat16
    dma = pltpu.SemaphoreType.DMA
    fixed = [
        pltpu.with_memory_space_constraint(a, pltpu.HBM)
        for a in (seeds, wavelet, sz, sy, sx, rz, ry, rx, courant, prev, now)
    ]
    held = pl.pallas_call(
        functools.partial(gather, nslab),
        out_shape=(
            pltpu.VMEM((2, nz, ny, nx), f32),
            pltpu.VMEM((nz, ny, nx), f32),
            pltpu.VMEM((2, nz, ny, nx), f32),
            pltpu.VMEM((STEPS, nz, ny, nx), f32),
            pltpu.VMEM((size, size), bf16),
            pltpu.VMEM((2 * nx, nx), bf16),
            pltpu.VMEM((2 * nrec, 2 * size), bf16),
            pltpu.VMEM((2, nrec, nx), f32),
            pltpu.VMEM((3, nrec, nx), f32),
        ),
        in_specs=[hbm] * 11,
        out_specs=(vmem,) * 9,
        scratch_shapes=[dma((nd,))] * 4
        + [dma((nd + 1,))] * 8
        + [pltpu.SMEM(a.shape, a.dtype) for a in (seeds, wavelet, sz, sy, sx, rz, ry, rx)]
        + [dma((11,))],
        compiler_params=pltpu.CompilerParams(
            collective_id=0, has_side_effects=True, vmem_limit_bytes=56 << 20
        ),
    )(*fixed)
    return pl.pallas_call(
        functools.partial(advance),
        out_shape=(
            jax.ShapeDtypeStruct((cz, cy, pw), f32),
            jax.ShapeDtypeStruct((2, cz, cy, nx), f32),
            jax.ShapeDtypeStruct((STEPS, 2, nrec), f32),
        ),
        in_specs=[hbm] * 2 + [vmem] * 9,
        out_specs=(hbm,) * 3,
        scratch_shapes=[
            pltpu.VMEM((2, nz, ny, nx), f32),
            pltpu.VMEM((2, 2, nz, ny, nx), f32),
            pltpu.VMEM((2, 2, nz, ny, 3 * nx), bf16),
            pltpu.VMEM((nz, ny, nx), f32),
            pltpu.VMEM((cz, cy, nx), f32),
            pltpu.VMEM((2, cz, cy, nx), f32),
            pltpu.VMEM((STEPS, 2, nrec), f32),
            pltpu.VMEM((nrec, nx), f32),
            pltpu.SMEM(rz.shape, rz.dtype),
            pltpu.SMEM(ry.shape, ry.dtype),
            dma((2,)),
            dma((4,)),
        ],
        compiler_params=pltpu.CompilerParams(vmem_limit_bytes=32 << 20),
    )(fixed[5], fixed[6], *held)


def solution(mesh):
    nslab = mesh.shape["slab"]
    reach = min(4, nslab - 1)
    win = min(nslab, 9)

    def shards(courant, prev, now, wavelet, sz, sy, sx, seeds, rz, ry, rx):
        cz, cy, pw = now.shape
        nx = courant.shape[2]
        split = 2 * pw == nx and pw % 128 == 0
        if split and nslab <= 4 and cy % 16 == 0:
            return whole(nslab, courant, prev, now, wavelet, sz, sy, sx, seeds, rz, ry, rx)
        if not split:
            prev = lax.all_gather(prev, "rep", axis=2, tiled=True)
            now = lax.all_gather(now, "rep", axis=2, tiled=True)
        width = now.shape[2]
        ny = 2 * cy
        zw = win * cz
        nd = 2 * reach
        nrec = rz.shape[0]
        tw = -(-nrec // 128) * 128
        group = 2 * nslab
        hbm = pl.BlockSpec(memory_space=pltpu.HBM)
        vmem = pl.BlockSpec(memory_space=pltpu.VMEM)
        f32 = jnp.float32
        dma = pltpu.SemaphoreType.DMA
        inc, wave, traces = pl.pallas_call(
            functools.partial(windowed, nslab, split, reach, win),
            out_shape=(
                pltpu.VMEM((cz, cy, width), f32),
                pltpu.VMEM((2, cz, cy, nx), f32),
                pltpu.VMEM((STEPS, 2, nrec), f32),
            ),
            in_specs=[hbm] * 11,
            out_specs=(vmem, vmem, vmem),
            scratch_shapes=[
                pltpu.VMEM((2, zw + 2 * cz, ny + 16, nx), f32),
                pltpu.VMEM((zw + 2 * cz, ny, nx), f32),
                pltpu.VMEM((2, 2, zw + 2 * cz, ny + 16, nx), f32),
                pltpu.VMEM((2, zw, ny, nx), f32),
                pltpu.VMEM((STEPS, zw, ny, nx), f32),
                pltpu.VMEM((3, zw, ny, nx), f32),
                pltpu.VMEM((3 * nx, nx), jnp.bfloat16),
                pltpu.VMEM((32, nx), f32),
                pltpu.VMEM((group, 8, tw), f32),
            ]
            + [dma((nd,))] * 4
            + [dma((nd + 1,))] * 8
            + [dma((group,))] * 2
            + [pltpu.SMEM(a.shape, a.dtype) for a in (wavelet, sz, sy, sx, seeds, rz, ry, rx)]
            + [dma((11,))],
            compiler_params=pltpu.CompilerParams(
                collective_id=0, has_side_effects=True, vmem_limit_bytes=60 << 20
            ),
        )(wavelet, sz, sy, sx, seeds, rz, ry, rx, courant, prev, now)
        if not split:
            pw0 = width // lax.axis_size("rep")
            inc = lax.dynamic_slice_in_dim(inc, lax.axis_index("rep") * pw0, pw0, 2)
        return inc, wave, traces

    return jax.shard_map(
        shards,
        mesh=mesh,
        in_specs=(
            P("slab", "sub", None),
            P(("shot", "slab"), "sub", "rep"),
            P(("shot", "slab"), "sub", "rep"),
            P(),
            P("shot"),
            P("shot"),
            P("shot"),
            P("rep"),
            P(),
            P(),
            P(),
        ),
        out_specs=(
            P(("shot", "slab"), "sub", "rep"),
            P("rep", ("shot", "slab"), "sub", None),
            P("shot", "rep", None),
        ),
        check_vma=False,
    )
```

```python
import functools
import jax
import jax.numpy as jnp
from jax import lax
from jax.experimental import pallas as pl
from jax.experimental.pallas import tpu as pltpu
from jax.sharding import PartitionSpec as P

STEPS = 4
COEF = (-205.0 / 72.0, 8.0 / 5.0, -1.0 / 5.0, 8.0 / 315.0, -1.0 / 560.0)
MESH = pl.DeviceIdType.MESH
HI = lax.Precision.HIGHEST


def windowed(
    nslab,
    split,
    reach,
    win,
    wav_in,
    sz_in,
    sy_in,
    sx_in,
    seeds_in,
    rz_in,
    ry_in,
    rx_in,
    cour,
    prev_in,
    now_in,
    inc_out,
    wave_out,
    trace_out,
    U,
    C,
    W,
    K,
    INJ,
    XP,
    BAND,
    ROWS,
    TB,
    zu_s,
    zu_r,
    zc_s,
    zc_r,
    xu_s,
    xu_r,
    yc_s,
    yc_r,
    su_s,
    su_r,
    sc_s,
    sc_r,
    t_s,
    t_r,
    wav,
    sz,
    sy,
    sx,
    seeds,
    rz,
    ry,
    rx,
    in_s,
):
    cz, cy, pw = now_in.shape
    nx = cour.shape[2]
    ny = 2 * cy
    zw = win * cz
    nrec = trace_out.shape[2]
    half = nx // 2
    shot = lax.axis_index("shot")
    s = lax.axis_index("slab")
    b = lax.axis_index("rep")
    c = lax.axis_index("sub")

    def base_of(t):
        return jnp.clip(t - reach, 0, nslab - win)

    base = base_of(s)

    barrier = pltpu.get_barrier_semaphore()
    others = []
    for d in range(1, 2 * nslab):
        other = lax.rem(s * 2 + c + d, 2 * nslab)
        others.append(other)
        pl.semaphore_signal(
            barrier,
            inc=1,
            device_id={"slab": lax.div(other, 2), "sub": lax.rem(other, 2)},
            device_id_type=MESH,
        )
    pl.semaphore_signal(barrier, inc=1, device_id={"shot": 1 - shot}, device_id_type=MESH)
    greeted = 2 * nslab
    if split:
        pl.semaphore_signal(barrier, inc=1, device_id={"rep": 1 - b}, device_id_type=MESH)
        greeted += 1

    def zpos(t, of):
        return cz + (t - of) * cz

    def ypos(c_):
        return pl.multiple_of(8 + c_ * cy, 8)

    def xpos(h, width):
        return pl.multiple_of(h * width, 128)

    own_z = zpos(s, base)
    xown = pl.ds(xpos(b, pw), pw) if split else pl.ds(0, pw)
    fetch = [
        pltpu.make_async_copy(src, dst, in_s.at[i])
        for i, (src, dst) in enumerate(
            [
                (now_in, U.at[0, pl.ds(own_z, cz), pl.ds(ypos(c), cy), xown]),
                (prev_in, U.at[1, pl.ds(own_z, cz), pl.ds(ypos(c), cy), xown]),
                (cour, C.at[pl.ds(own_z, cz), pl.ds(pl.multiple_of(c * cy, 8), cy), :]),
                (seeds_in, seeds),
                (wav_in, wav),
                (sz_in, sz),
                (sy_in, sy),
                (sx_in, sx),
                (rz_in, rz),
                (ry_in, ry),
                (rx_in, rx),
            ]
        )
    ]
    for copy in fetch:
        copy.start()

    def u_piece(t, of, h):
        xs = pl.ds(xpos(h, pw), pw) if split else pl.ds(0, pw)
        return U.at[:, pl.ds(zpos(t, of), cz), pl.ds(ypos(c), cy), xs]

    def near(rows, c_):
        return pl.multiple_of((1 - c_) * (cy - rows), 8)

    def u_near(t, d, c_):
        rows = max(8, min(cy, -(-(16 - 4 * abs(d)) // 8) * 8))
        fields = pl.ds(0, 1 if abs(d) >= 3 else 2)
        return U.at[fields, pl.ds(zpos(t, base), cz), pl.ds(ypos(c_) + near(rows, c_), rows), :]

    def c_near(t, d, c_):
        rows = min(cy, -(-(12 - 4 * abs(d)) // 8) * 8)
        start = pl.multiple_of(c_ * cy, 8) + near(rows, c_)
        return C.at[pl.ds(zpos(t, base), cz), pl.ds(start, rows), :]

    def c_rows(t, of, c_, h):
        rows = pl.ds(pl.multiple_of(c_ * cy, 8), cy)
        xs = pl.ds(0, nx) if h is None else pl.ds(xpos(h, half), half)
        return C.at[pl.ds(zpos(t, of), cz), rows, xs]

    def rcopy(src, dst, ss, rs, device):
        return pltpu.make_async_remote_copy(
            src_ref=src, dst_ref=dst, send_sem=ss, recv_sem=rs, device_id=device, device_id_type=MESH
        )

    dists = []
    for d in range(reach, 0, -1):
        dists += [d, -d]

    for copy in fetch[:3]:
        copy.wait()
    pl.semaphore_wait(barrier, greeted)

    def z_copies(i, d):
        t = s + d
        of = base_of(t)
        return (
            rcopy(u_piece(s, base, b), u_piece(s, of, b), zu_s.at[i], zu_r.at[i], {"slab": t}),
            rcopy(
                c_rows(s, base, c, shot),
                c_rows(s, of, c, shot),
                zc_s.at[i],
                zc_r.at[i],
                {"slab": t},
            ),
        )

    def inside(t):
        return (t >= 0) & (t < nslab)

    def x_copy(i, t, h):
        return rcopy(u_piece(t, base, h), u_piece(t, base, h), xu_s.at[i], xu_r.at[i], {"rep": 1 - b})

    def y_copy(i, t, h):
        return rcopy(
            c_rows(t, base, c, h), c_rows(t, base, c, h), yc_s.at[i], yc_r.at[i], {"shot": 1 - shot}
        )

    def sub_u(i, t, d, mine):
        row = u_near(t, d, c if mine else 1 - c)
        return rcopy(row, row, su_s.at[i], su_r.at[i], {"sub": 1 - c})

    def sub_c(i, t, d, mine):
        row = c_near(t, d, c if mine else 1 - c)
        return rcopy(row, row, sc_s.at[i], sc_r.at[i], {"sub": 1 - c})

    if split:
        x_copy(0, s, b).start()
    for i, d in enumerate(dists):

        @pl.when(inside(s + d))
        def _():
            u_copy, c_copy = z_copies(i, d)
            u_copy.start()
            c_copy.start()

    sub_c(0, s, 0, True).start()

    wp = W.shape[-2]
    for buf in range(2):
        U[buf, pl.ds(0, cz)] = jnp.zeros((cz, wp, nx), jnp.float32)
        U[buf, pl.ds(cz + zw, cz)] = jnp.zeros((cz, wp, nx), jnp.float32)
        U[buf, pl.ds(cz, zw), pl.ds(0, 8), :] = jnp.zeros((zw, 8, nx), jnp.float32)
        U[buf, pl.ds(cz, zw), pl.ds(8 + ny, 8), :] = jnp.zeros((zw, 8, nx), jnp.float32)
        for r in range(2):
            W[buf, r, pl.ds(0, cz)] = jnp.zeros((cz, wp, nx), jnp.float32)
            W[buf, r, pl.ds(cz + zw, cz)] = jnp.zeros((cz, wp, nx), jnp.float32)
            W[buf, r, pl.ds(cz, zw), pl.ds(0, 8), :] = jnp.zeros((zw, 8, nx), jnp.float32)
            W[buf, r, pl.ds(cz, zw), pl.ds(8 + ny, 8), :] = jnp.zeros((zw, 8, nx), jnp.float32)

    gap = jnp.abs(
        lax.broadcasted_iota(jnp.int32, (nx, nx), 0) - lax.broadcasted_iota(jnp.int32, (nx, nx), 1)
    )
    band = jnp.zeros((nx, nx), jnp.float32)
    for k in range(1, 5):
        band = jnp.where(gap == k, COEF[k], band)
    high = band.astype(jnp.bfloat16)
    BAND[pl.ds(0, nx), :] = high
    BAND[pl.ds(nx, nx), :] = high
    BAND[pl.ds(2 * nx, nx), :] = (band - high.astype(jnp.float32)).astype(jnp.bfloat16)

    for copy in fetch[3:]:
        copy.wait()
    ycoord = lax.broadcasted_iota(jnp.int32, (ny, nx), 0)
    xcoord = lax.broadcasted_iota(jnp.int32, (ny, nx), 1)
    flat = ycoord * 19349663 + xcoord * 83492791

    @pl.loop(0, zw)
    def _(z):
        for r in range(2):
            h = flat + (seeds[r] * 668265263 + (base * cz + z) * 73856093)
            h = jnp.bitwise_xor(h, jnp.right_shift(h, 15))
            h = h * 1274126177
            h = jnp.bitwise_xor(h, jnp.right_shift(h, 13))
            f = jnp.bitwise_and(h, 65535).astype(jnp.float32)
            K[r, z] = f * (0.8 / 65535.0) - 0.4

    nsrc = sx.shape[0]
    lane = lax.broadcasted_iota(jnp.int32, (1, nsrc), 1)
    place = jnp.zeros((1, nsrc), jnp.int32)
    column = jnp.zeros((nsrc, nx), jnp.int32)
    ksub = lax.broadcasted_iota(jnp.int32, (nsrc, nx), 0)
    for k in range(nsrc):
        place = jnp.where(lane == k, (sz[k] - base * cz) * ny + sy[k], place)
        column = jnp.where(ksub == k, sx[k], column)
    hit_x = jnp.where(lax.broadcasted_iota(jnp.int32, (nsrc, nx), 1) == column, 1.0, 0.0)
    row_id = lax.broadcasted_iota(jnp.int32, (zw * ny, nsrc), 0)
    hit = row_id == place
    for n in range(STEPS):
        amounts = jnp.zeros((1, nsrc), jnp.float32)
        for k in range(nsrc):
            amounts = jnp.where(lane == k, wav[n, k], amounts)
        rows = jnp.where(hit, amounts, 0.0)
        INJ[n] = jnp.dot(rows, hit_x, precision=HI, preferred_element_type=jnp.float32).reshape(
            zw, ny, nx
        )

    def hand_over(i, d):
        @pl.when(inside(s - d))
        def _():
            t = s - d
            y_copy(i + 1, t, 1 - shot).wait_recv()
            if abs(d) < 3:
                sub_c(i + 1, t, d, True).start()
            if split:
                x_copy(i + 1, t, 1 - b).wait_recv()
            if abs(d) < 4:
                sub_u(i + 1, t, d, True).start()

    if split:
        x_copy(0, s, 1 - b).wait_recv()
    sub_u(0, s, 0, True).start()
    for i, d in enumerate(dists):

        @pl.when(inside(s - d))
        def _():
            t = s - d
            mine = u_piece(t, base, b)
            rcopy(mine, mine, zu_s.at[i], zu_r.at[i], {"slab": s}).wait_recv()
            if split:
                x_copy(i + 1, t, b).start()
            mine = c_rows(t, base, c, shot)
            rcopy(mine, mine, zc_s.at[i], zc_r.at[i], {"slab": s}).wait_recv()
            y_copy(i + 1, t, shot).start()

    for i, d in enumerate(dists):
        hand_over(i, d)

    sub_c(0, s, 0, False).wait_recv()
    sub_u(0, s, 0, False).wait_recv()
    for i, d in enumerate(dists):

        @pl.when(inside(s - d))
        def _():
            if abs(d) < 3:
                sub_c(i + 1, s - d, d, False).wait_recv()
            if abs(d) < 4:
                sub_u(i + 1, s - d, d, False).wait_recv()

    if split:
        x_copy(0, s, b).wait_send()
    sub_c(0, s, 0, True).wait_send()
    sub_u(0, s, 0, True).wait_send()
    for i, d in enumerate(dists):

        @pl.when(inside(s + d))
        def _():
            u_copy, c_copy = z_copies(i, d)
            u_copy.wait_send()
            c_copy.wait_send()

        @pl.when(inside(s - d))
        def _():
            t = s - d
            if split:
                x_copy(i + 1, t, b).wait_send()
            y_copy(i + 1, t, shot).wait_send()
            if abs(d) < 3:
                sub_c(i + 1, t, d, True).wait_send()
            if abs(d) < 4:
                sub_u(i + 1, t, d, True).wait_send()

    core = (s - base) * cz
    j0 = (s * 2 + c) * 4

    def step(n, y0, rows):
        now, before = n % 2, 1 - n % 2
        left = STEPS - 1 - n
        nz = min(zw, cz + 8 * left)
        z0 = jnp.clip(core - 4 * left, 0, zw - nz)
        wnow, wnext = (n + 1) % 2, n % 2
        ys = pl.ds(8 + y0, rows)
        yc = pl.ds(y0, rows)

        def across(ref):
            v = ref[pl.ds(cz + z0, nz), ys, :].reshape(nz * rows, nx)
            high = v.astype(jnp.bfloat16)
            low = (v - high.astype(jnp.float32)).astype(jnp.bfloat16)
            both = jnp.concatenate([high, low, high], axis=1)
            out = jnp.dot(both, BAND[...], preferred_element_type=jnp.float32)
            return out.reshape(nz, rows, nx)

        XP[0, pl.ds(0, nz), pl.ds(0, rows), :] = across(U.at[now])
        if n > 0:
            for r in range(2):
                XP[1 + r, pl.ds(0, nz), pl.ds(0, rows), :] = across(W.at[wnow, r])

        @pl.loop(0, nz, unroll=4)
        def _(i):
            z = z0 + i
            p = z + cz
            speed = C[p, yc, :]
            speed = speed * speed

            def lap(ref, mid, part):
                acc = part + (3.0 * COEF[0]) * mid
                for k in range(1, 5):
                    acc = acc + COEF[k] * (
                        (ref[p + k, ys, :] + ref[p - k, ys, :])
                        + (ref[p, pl.ds(8 + y0 + k, rows), :] + ref[p, pl.ds(8 + y0 - k, rows), :])
                    )
                return acc

            mid = U[now, p, ys, :]
            delta = speed * lap(U.at[now], mid, XP[0, i, pl.ds(0, rows), :]) + INJ[n, z, yc, :]
            U[before, p, ys, :] = 2.0 * mid - U[before, p, ys, :] + delta
            for r in range(2):
                term = K[r, z, yc, :] * delta
                if n > 0:
                    mid = W[wnow, r, p, ys, :]
                    term = term + speed * lap(W.at[wnow, r], mid, XP[1 + r, i, pl.ds(0, rows), :])
                    term = term + 2.0 * mid
                if n > 1:
                    term = term - W[wnext, r, p, ys, :]
                W[wnext, r, p, ys, :] = term

        for i in range(4):
            zj = rz[j0 + i] - base * cz + cz
            yj = ry[j0 + i] + 8
            for r in range(2):
                ROWS[pl.ds(i * 8 + n * 2 + r, 1), :] = W[wnext, r, zj, pl.ds(yj, 1), :]

    step(0, 0, ny)
    for side in range(2):

        @pl.when(c == side)
        def _():
            for n in range(1, STEPS):
                rows = min(ny, cy + 8 * -(-(STEPS - 1 - n) // 2))
                step(n, side * (ny - rows), rows)

    tw = TB.shape[2]
    lane_x = lax.broadcasted_iota(jnp.int32, (8, nx), 1)
    lane_j = lax.broadcasted_iota(jnp.int32, (8, tw), 1)
    tile = jnp.zeros((8, tw), jnp.float32)
    for i in range(4):
        picked = jnp.where(lane_x == rx[j0 + i], ROWS[pl.ds(i * 8, 8), :], 0.0)
        picked = jnp.sum(picked, axis=1, keepdims=True)
        tile = jnp.where(lane_j == j0 + i, picked, tile)
    me = s * 2 + c
    TB[me] = tile

    def t_copy(d, src, target):
        return rcopy(
            TB.at[src],
            TB.at[src],
            t_s.at[d],
            t_r.at[d],
            {"slab": lax.div(target, 2), "sub": lax.rem(target, 2)},
        )

    for d in range(1, 2 * nslab):
        t_copy(d, me, others[d - 1]).start()
    last = (STEPS - 1) % 2
    wave_out[...] = W[last, :, pl.ds(cz + core, cz), pl.ds(ypos(c), cy), :]
    if split:
        inc_out[...] = U[STEPS % 2, pl.ds(cz + core, cz), pl.ds(ypos(c), cy), xown]
    else:
        inc_out[...] = U[STEPS % 2, pl.ds(cz + core, cz), pl.ds(ypos(c), cy), :]

    for d in range(1, 2 * nslab):
        source = lax.rem(me + 2 * nslab - d, 2 * nslab)
        t_copy(d, source, others[d - 1]).wait_recv()
        tile = tile + TB[source]
    for d in range(1, 2 * nslab):
        t_copy(d, me, others[d - 1]).wait_send()
    for n in range(STEPS):
        trace_out[n] = tile[2 * n : 2 * n + 2, :nrec]


SCALE = 5040.0 / 4096.0
TAPS = tuple(v / 4096.0 for v in (-43050.0, 8064.0, -1008.0, 128.0, -9.0))


def tap_of(gap):
    out = jnp.where(gap == 1, TAPS[1], 0.0)
    for k in range(2, 5):
        out = jnp.where(gap == k, TAPS[k], out)
    return out


def gather(
    nslab,
    seeds_in,
    wav_in,
    sz_in,
    sy_in,
    sx_in,
    rz_in,
    ry_in,
    rx_in,
    cour,
    prev_in,
    now_in,
    U,
    C,
    K,
    INJ,
    A,
    B2,
    G2,
    RX,
    RR,
    zu_s,
    zu_r,
    zc_s,
    zc_r,
    xu_s,
    xu_r,
    yc_s,
    yc_r,
    su_s,
    su_r,
    sc_s,
    sc_r,
    seeds,
    wav,
    sz,
    sy,
    sx,
    rz,
    ry,
    rx,
    in_s,
):
    cz, cy, pw = now_in.shape
    nz, ny, nx = C.shape
    size = nz * ny
    half = nx // 2
    shot = lax.axis_index("shot")
    s = lax.axis_index("slab")
    b = lax.axis_index("rep")
    c = lax.axis_index("sub")

    barrier = pltpu.get_barrier_semaphore()
    for d in range(1, nslab):
        pl.semaphore_signal(
            barrier, inc=1, device_id={"slab": lax.rem(s + d, nslab)}, device_id_type=MESH
        )
    for other in ({"shot": 1 - shot}, {"rep": 1 - b}, {"sub": 1 - c}):
        pl.semaphore_signal(barrier, inc=1, device_id=other, device_id_type=MESH)
    greeted = nslab + 2

    def rows_of(c_):
        return pl.ds(pl.multiple_of(c_ * cy, 8), cy)

    def lanes_of(h):
        return pl.ds(pl.multiple_of(h * half, 128), half)

    def u_at(t, c_, h):
        return U.at[:, pl.ds(t * cz, cz), rows_of(c_), lanes_of(h)]

    def c_at(t, c_, h):
        return C.at[pl.ds(t * cz, cz), rows_of(c_), lanes_of(h)]

    def c_full(t, c_):
        return C.at[pl.ds(t * cz, cz), rows_of(c_), :]

    fetch = [
        pltpu.make_async_copy(src, dst, in_s.at[i])
        for i, (src, dst) in enumerate(
            [
                (now_in, U.at[0, pl.ds(s * cz, cz), rows_of(c), lanes_of(b)]),
                (prev_in, U.at[1, pl.ds(s * cz, cz), rows_of(c), lanes_of(b)]),
                (cour, c_full(s, c)),
                (seeds_in, seeds),
                (wav_in, wav),
                (sz_in, sz),
                (sy_in, sy),
                (sx_in, sx),
                (rz_in, rz),
                (ry_in, ry),
                (rx_in, rx),
            ]
        )
    ]
    for copy in fetch:
        copy.start()

    def rcopy(piece, ss, rs, device):
        return pltpu.make_async_remote_copy(
            src_ref=piece,
            dst_ref=piece,
            send_sem=ss,
            recv_sem=rs,
            device_id=device,
            device_id_type=MESH,
        )

    dists = []
    for d in range(nslab - 1, 0, -1):
        dists += [d, -d]

    def inside(t):
        return (t >= 0) & (t < nslab)

    def z_u(i, t, target):
        return rcopy(u_at(t, c, b), zu_s.at[i], zu_r.at[i], {"slab": target})

    def z_c(i, t, target):
        return rcopy(c_at(t, c, shot), zc_s.at[i], zc_r.at[i], {"slab": target})

    def x_u(i, t, h):
        return rcopy(u_at(t, c, h), xu_s.at[i], xu_r.at[i], {"rep": 1 - b})

    def y_c(i, t, h):
        return rcopy(c_at(t, c, h), yc_s.at[i], yc_r.at[i], {"shot": 1 - shot})

    def sub_u(i, t, c_, h, kind):
        k = 2 * i + kind
        return rcopy(u_at(t, c_, h), su_s.at[k], su_r.at[k], {"sub": 1 - c})

    def sub_c(i, t, c_):
        return rcopy(c_full(t, c_), sc_s.at[i], sc_r.at[i], {"sub": 1 - c})

    for copy in fetch[:3]:
        copy.wait()
    pl.semaphore_wait(barrier, greeted)

    x_u(0, s, b).start()
    for i, d in enumerate(dists):

        @pl.when(inside(s + d))
        def _():
            z_u(i, s, s + d).start()
            z_c(i, s, s + d).start()

    sub_c(0, s, c).start()
    sub_u(0, s, c, b, 0).start()

    rowy = lax.broadcasted_iota(jnp.int32, (ny, size), 0)
    col = lax.broadcasted_iota(jnp.int32, (ny, size), 1)
    colz, coly = col // ny, col % ny

    @pl.loop(0, nz)
    def _(z):
        gap = jnp.where(
            rowy == coly, jnp.abs(z - colz), jnp.where(z == colz, jnp.abs(rowy - coly), 0)
        )
        A[pl.ds(pl.multiple_of(z * ny, 16), ny), :] = tap_of(gap).astype(jnp.bfloat16)

    gap = jnp.abs(
        lax.broadcasted_iota(jnp.int32, (nx, nx), 0) - lax.broadcasted_iota(jnp.int32, (nx, nx), 1)
    )
    taps = tap_of(gap).astype(jnp.bfloat16)
    B2[pl.ds(0, nx), :] = taps
    B2[pl.ds(nx, nx), :] = taps

    for copy in fetch[3:]:
        copy.wait()
    ycoord = lax.broadcasted_iota(jnp.int32, (ny, nx), 0)
    xcoord = lax.broadcasted_iota(jnp.int32, (ny, nx), 1)
    flat = ycoord * 19349663 + xcoord * 83492791

    @pl.loop(0, nz)
    def _(z):
        for r in range(2):
            h = flat + (seeds[r] * 668265263 + z * 73856093)
            h = jnp.bitwise_xor(h, jnp.right_shift(h, 15))
            h = h * 1274126177
            h = jnp.bitwise_xor(h, jnp.right_shift(h, 13))
            f = jnp.bitwise_and(h, 65535).astype(jnp.float32)
            K[r, z] = f * (0.8 / 65535.0) - 0.4

    nsrc = sx.shape[0]
    lane = lax.broadcasted_iota(jnp.int32, (1, nsrc), 1)
    place = jnp.zeros((1, nsrc), jnp.int32)
    column = jnp.zeros((nsrc, nx), jnp.int32)
    ksub = lax.broadcasted_iota(jnp.int32, (nsrc, nx), 0)
    for k in range(nsrc):
        place = jnp.where(lane == k, sz[k] * ny + sy[k], place)
        column = jnp.where(ksub == k, sx[k], column)
    hit_x = jnp.where(lax.broadcasted_iota(jnp.int32, (nsrc, nx), 1) == column, 1.0, 0.0)
    hit = lax.broadcasted_iota(jnp.int32, (size, nsrc), 0) == place
    for n in range(STEPS):
        amounts = jnp.zeros((1, nsrc), jnp.float32)
        for k in range(nsrc):
            amounts = jnp.where(lane == k, wav[n, k], amounts)
        rows = jnp.where(hit, amounts, 0.0)
        INJ[n] = jnp.dot(rows, hit_x, precision=HI, preferred_element_type=jnp.float32).reshape(
            nz, ny, nx
        )

    nrec = rz.shape[0]
    sub_j = lax.broadcasted_iota(jnp.int32, (nrec, 128), 0)
    jz = jnp.zeros((nrec, 128), jnp.int32)
    jy = jnp.zeros((nrec, 128), jnp.int32)
    jx = jnp.zeros((nrec, 128), jnp.int32)
    for j in range(nrec):
        jz = jnp.where(sub_j == j, rz[j], jz)
        jy = jnp.where(sub_j == j, ry[j], jy)
        jx = jnp.where(sub_j == j, rx[j], jx)
    lane_j = lax.broadcasted_iota(jnp.int32, (nrec, 128), 1)
    for q in range(size // 128):
        z, y = (q * 128 + lane_j) // ny, (q * 128 + lane_j) % ny
        dz, dy = jnp.abs(z - jz), jnp.abs(y - jy)
        here = jnp.where(dz + dy == 0, 1.0, 0.0).astype(jnp.bfloat16)
        gap = jnp.where(dy == 0, dz, jnp.where(dz == 0, dy, 0))
        near = tap_of(gap).astype(jnp.bfloat16)
        for part in range(2):
            G2[pl.ds(0, nrec), pl.ds(part * size + q * 128, 128)] = here
            G2[pl.ds(nrec, nrec), pl.ds(part * size + q * 128, 128)] = near
    for q in range(nx // 128):
        gap = jnp.abs(q * 128 + lane_j - jx)
        RX[0, :, pl.ds(q * 128, 128)] = jnp.where(gap == 0, 1.0, 0.0)
        RX[1, :, pl.ds(q * 128, 128)] = tap_of(gap) + jnp.where(gap == 0, TAPS[0], 0.0)
    for j in range(nrec):
        for r in range(2):
            RR[r, pl.ds(j, 1), :] = K[r, rz[j], pl.ds(ry[j], 1), :]
        RR[2, pl.ds(j, 1), :] = INJ[STEPS - 1, rz[j], pl.ds(ry[j], 1), :]

    x_u(0, s, 1 - b).wait_recv()
    sub_u(0, s, c, 1 - b, 1).start()
    for i, d in enumerate(dists):

        @pl.when(inside(s - d))
        def _():
            z_u(i, s - d, s).wait_recv()
            x_u(i + 1, s - d, b).start()
            sub_u(i + 1, s - d, c, b, 0).start()
            z_c(i, s - d, s).wait_recv()
            y_c(i + 1, s - d, shot).start()

    for i, d in enumerate(dists):

        @pl.when(inside(s - d))
        def _():
            y_c(i + 1, s - d, 1 - shot).wait_recv()
            sub_c(i + 1, s - d, c).start()
            x_u(i + 1, s - d, 1 - b).wait_recv()
            sub_u(i + 1, s - d, c, 1 - b, 1).start()

    sub_c(0, s, 1 - c).wait_recv()
    sub_u(0, s, 1 - c, b, 0).wait_recv()
    sub_u(0, s, 1 - c, 1 - b, 1).wait_recv()
    for i, d in enumerate(dists):

        @pl.when(inside(s - d))
        def _():
            sub_c(i + 1, s - d, 1 - c).wait_recv()
            sub_u(i + 1, s - d, 1 - c, b, 0).wait_recv()
            sub_u(i + 1, s - d, 1 - c, 1 - b, 1).wait_recv()

    x_u(0, s, b).wait_send()
    sub_c(0, s, c).wait_send()
    sub_u(0, s, c, b, 0).wait_send()
    sub_u(0, s, c, 1 - b, 1).wait_send()
    for i, d in enumerate(dists):

        @pl.when(inside(s + d))
        def _():
            z_u(i, s, s + d).wait_send()
            z_c(i, s, s + d).wait_send()

        @pl.when(inside(s - d))
        def _():
            x_u(i + 1, s - d, b).wait_send()
            y_c(i + 1, s - d, shot).wait_send()
            sub_c(i + 1, s - d, c).wait_send()
            sub_u(i + 1, s - d, c, b, 0).wait_send()
            sub_u(i + 1, s - d, c, 1 - b, 1).wait_send()


def advance(
    rz_in,
    ry_in,
    U0,
    C,
    K,
    INJ,
    A,
    B2,
    G2,
    RX,
    RR,
    inc_out,
    wave_out,
    trace_out,
    U,
    W,
    HL,
    SP,
    INC,
    WAVE,
    TR,
    RC,
    rz,
    ry,
    in_s,
    out_s,
):
    cz, cy, pw = inc_out.shape
    nz, ny, nx = C.shape
    size = nz * ny
    nrec = rz.shape[0]
    s = lax.axis_index("slab")
    b = lax.axis_index("rep")
    c = lax.axis_index("sub")
    fetch = [
        pltpu.make_async_copy(src, dst, in_s.at[i])
        for i, (src, dst) in enumerate([(rz_in, rz), (ry_in, ry)])
    ]
    for copy in fetch:
        copy.start()

    slabs = nz // cz
    rows = cz * ny

    def split(buf, field, z, v):
        high = v.astype(jnp.bfloat16)
        HL[buf, 0, z, :, pl.ds(field * nx, nx)] = high
        HL[buf, 1, z, :, pl.ds(field * nx, nx)] = (v - high.astype(jnp.float32)).astype(
            jnp.bfloat16
        )

    def parts(buf, field, z0, count):
        xs = pl.ds(field * nx, nx)
        return [HL[buf, p, pl.ds(z0, count), :, xs].reshape(count * ny, nx) for p in range(2)]

    def lap_slab(buf, field, t):
        lo, hi = max(t - 1, 0), min(t + 2, slabs)
        a = A[pl.ds(t * rows, rows), pl.ds(lo * rows, (hi - lo) * rows)]
        lhs = jnp.concatenate([a, a] + parts(buf, field, t * cz, cz), axis=1)
        rhs = jnp.concatenate(parts(buf, field, lo * cz, (hi - lo) * cz) + [B2[...]], axis=0)
        return jnp.dot(lhs, rhs, preferred_element_type=jnp.float32)

    def at_receivers(buf, field, count):
        rhs = jnp.concatenate(parts(buf, field, 0, nz), axis=0)
        return jnp.dot(G2[pl.ds(0, count), :], rhs, preferred_element_type=jnp.float32)

    def pick(rows):
        return jnp.sum(rows, axis=1, keepdims=True)

    @pl.loop(0, nz, unroll=2)
    def _(z):
        split(0, 0, z, U0[0, z])
        SP[z] = C[z] * C[z] * (1.0 / SCALE)

    seen = {}
    for n in range(STEPS - 1):
        now, before = n % 2, 1 - n % 2
        wnow, wnext = (n + 1) % 2, n % 2
        buf, nbuf = n % 2, 1 - n % 2
        unow = U0 if n == 0 else U
        uold = U0 if n < 2 else U
        for t in range(slabs):
            laps = [lap_slab(buf, f, t) for f in range(3 if n > 0 else 1)]
            for i in range(cz):
                z = t * cz + i
                part = [v[i * ny : i * ny + ny] for v in laps]
                speed = SP[z]
                mid = unow[now, z]
                delta = speed * (part[0] + TAPS[0] * mid) + INJ[n, z]
                v = 2.0 * mid - uold[before, z] + delta
                U[before, z] = v
                split(nbuf, 0, z, v)
                for r in range(2):
                    v = K[r, z] * delta
                    if n > 0:
                        mid = W[wnow, r, z]
                        v = v + (speed * (part[1 + r] + TAPS[0] * mid) + 2.0 * mid)
                    if n > 1:
                        v = v - W[wnext, r, z]
                    W[wnext, r, z] = v
                    split(nbuf, 1 + r, z, v)
        if n > 0:
            for r in range(2):
                seen[n, r] = pick(at_receivers(buf, 1 + r, nrec) * RX[0])

    for copy in fetch:
        copy.wait()
    for j in range(nrec):
        RC[pl.ds(j, 1), :] = SP[rz[j], pl.ds(ry[j], 1), :]

    n = STEPS - 1
    now, before = n % 2, 1 - n % 2
    wnow, wnext = (n + 1) % 2, n % 2
    own_z = pl.ds(s * cz, cz)
    own_y = pl.ds(pl.multiple_of(c * cy, 16), cy)
    lanes = pl.ds(pl.multiple_of(b * pw, 128), pw)
    area = cz * cy

    def own(ref, *lead):
        return ref[(*lead, own_z, own_y, slice(None))].reshape(area, nx)

    first = pl.multiple_of(s * cz * ny + c * cy, 16)
    own_a = jnp.concatenate(
        [A[pl.ds(pl.multiple_of(first + z * ny, 16), cy), :] for z in range(cz)], axis=0
    )
    speed = own(SP)
    speed_j = pick(RC[...] * RX[0])

    def last(field, mid):
        high, low = parts(n % 2, field, 0, nz)
        xs = pl.ds(field * nx, nx)
        mine = [HL[n % 2, p, own_z, own_y, xs].reshape(area, nx) for p in range(2)]
        lhs = jnp.concatenate([jnp.concatenate([own_a, own_a], axis=1), G2[...]], axis=0)
        out = jnp.dot(
            lhs, jnp.concatenate([high, low], axis=0), preferred_element_type=jnp.float32
        )
        across = jnp.dot(
            jnp.concatenate(mine, axis=1), B2[...], preferred_element_type=jnp.float32
        )
        here = out[area : area + nrec]
        lap_j = pick(out[area + nrec :] * RX[0] + here * RX[1])
        return out[:area] + across + TAPS[0] * mid, pick(here * RX[0]), lap_j

    mid = own(U, now)
    lap, _, lap_j = last(0, mid)
    delta = speed * lap + own(INJ, n)
    INC[...] = (2.0 * mid - own(U, before) + delta).reshape(cz, cy, nx)
    outs = [pltpu.make_async_copy(INC.at[:, :, lanes], inc_out, out_s.at[0])]
    outs[0].start()
    delta_j = speed_j * lap_j + pick(RR[2] * RX[0])
    for r in range(2):
        mid = own(W, wnow, r)
        lap, here, lap_j = last(1 + r, mid)
        v = own(K, r) * delta + speed * lap + 2.0 * mid - own(W, wnext, r)
        WAVE[r] = v.reshape(cz, cy, nx)
        outs.append(pltpu.make_async_copy(WAVE.at[r], wave_out.at[r], out_s.at[1 + r]))
        outs[-1].start()
        seen[n, r] = here
        kick = pick(RR[r] * RX[0]) * delta_j
        seen[n + 1, r] = 2.0 * here - seen[n - 1, r] + speed_j * lap_j + kick
    lane = lax.broadcasted_iota(jnp.int32, (nrec, 128), 1)
    table = jnp.zeros((nrec, 128), jnp.float32)
    for n in range(STEPS):
        for r in range(2):
            table = jnp.where(lane == 2 * n + r, seen[n + 1, r], table)
    table = table.T
    for n in range(STEPS):
        TR[n] = table[2 * n : 2 * n + 2, :nrec]
    outs.append(pltpu.make_async_copy(TR, trace_out, out_s.at[3]))
    outs[-1].start()
    for copy in outs:
        copy.wait()


def whole(nslab, courant, prev, now, wavelet, sz, sy, sx, seeds, rz, ry, rx):
    cz, cy, pw = now.shape
    nx = courant.shape[2]
    nz, ny = nslab * cz, 2 * cy
    size = nz * ny
    nrec = rz.shape[0]
    nd = 2 * (nslab - 1)
    hbm = pl.BlockSpec(memory_space=pltpu.HBM)
    vmem = pl.BlockSpec(memory_space=pltpu.VMEM)
    f32, bf16 = jnp.float32, jnp.bfloat16
    dma = pltpu.SemaphoreType.DMA
    fixed = [
        pltpu.with_memory_space_constraint(a, pltpu.HBM)
        for a in (seeds, wavelet, sz, sy, sx, rz, ry, rx, courant, prev, now)
    ]
    held = pl.pallas_call(
        functools.partial(gather, nslab),
        out_shape=(
            pltpu.VMEM((2, nz, ny, nx), f32),
            pltpu.VMEM((nz, ny, nx), f32),
            pltpu.VMEM((2, nz, ny, nx), f32),
            pltpu.VMEM((STEPS, nz, ny, nx), f32),
            pltpu.VMEM((size, size), bf16),
            pltpu.VMEM((2 * nx, nx), bf16),
            pltpu.VMEM((2 * nrec, 2 * size), bf16),
            pltpu.VMEM((2, nrec, nx), f32),
            pltpu.VMEM((3, nrec, nx), f32),
        ),
        in_specs=[hbm] * 11,
        out_specs=(vmem,) * 9,
        scratch_shapes=[dma((nd,))] * 4
        + [dma((nd + 1,))] * 4
        + [dma((2 * nd + 2,))] * 2
        + [dma((nd + 1,))] * 2
        + [pltpu.SMEM(a.shape, a.dtype) for a in (seeds, wavelet, sz, sy, sx, rz, ry, rx)]
        + [dma((11,))],
        compiler_params=pltpu.CompilerParams(
            collective_id=0, has_side_effects=True, vmem_limit_bytes=56 << 20
        ),
    )(*fixed)
    return pl.pallas_call(
        functools.partial(advance),
        out_shape=(
            jax.ShapeDtypeStruct((cz, cy, pw), f32),
            jax.ShapeDtypeStruct((2, cz, cy, nx), f32),
            jax.ShapeDtypeStruct((STEPS, 2, nrec), f32),
        ),
        in_specs=[hbm] * 2 + [vmem] * 9,
        out_specs=(hbm,) * 3,
        scratch_shapes=[
            pltpu.VMEM((2, nz, ny, nx), f32),
            pltpu.VMEM((2, 2, nz, ny, nx), f32),
            pltpu.VMEM((2, 2, nz, ny, 3 * nx), bf16),
            pltpu.VMEM((nz, ny, nx), f32),
            pltpu.VMEM((cz, cy, nx), f32),
            pltpu.VMEM((2, cz, cy, nx), f32),
            pltpu.VMEM((STEPS, 2, nrec), f32),
            pltpu.VMEM((nrec, nx), f32),
            pltpu.SMEM(rz.shape, rz.dtype),
            pltpu.SMEM(ry.shape, ry.dtype),
            dma((2,)),
            dma((4,)),
        ],
        compiler_params=pltpu.CompilerParams(vmem_limit_bytes=32 << 20),
    )(fixed[5], fixed[6], *held)


def solution(mesh):
    nslab = mesh.shape["slab"]
    reach = min(4, nslab - 1)
    win = min(nslab, 9)

    def shards(courant, prev, now, wavelet, sz, sy, sx, seeds, rz, ry, rx):
        cz, cy, pw = now.shape
        nx = courant.shape[2]
        split = 2 * pw == nx and pw % 128 == 0
        if split and nslab <= 4 and cy % 16 == 0:
            return whole(nslab, courant, prev, now, wavelet, sz, sy, sx, seeds, rz, ry, rx)
        if not split:
            prev = lax.all_gather(prev, "rep", axis=2, tiled=True)
            now = lax.all_gather(now, "rep", axis=2, tiled=True)
        width = now.shape[2]
        ny = 2 * cy
        zw = win * cz
        nd = 2 * reach
        nrec = rz.shape[0]
        tw = -(-nrec // 128) * 128
        group = 2 * nslab
        hbm = pl.BlockSpec(memory_space=pltpu.HBM)
        vmem = pl.BlockSpec(memory_space=pltpu.VMEM)
        f32 = jnp.float32
        dma = pltpu.SemaphoreType.DMA
        inc, wave, traces = pl.pallas_call(
            functools.partial(windowed, nslab, split, reach, win),
            out_shape=(
                pltpu.VMEM((cz, cy, width), f32),
                pltpu.VMEM((2, cz, cy, nx), f32),
                pltpu.VMEM((STEPS, 2, nrec), f32),
            ),
            in_specs=[hbm] * 11,
            out_specs=(vmem, vmem, vmem),
            scratch_shapes=[
                pltpu.VMEM((2, zw + 2 * cz, ny + 16, nx), f32),
                pltpu.VMEM((zw + 2 * cz, ny, nx), f32),
                pltpu.VMEM((2, 2, zw + 2 * cz, ny + 16, nx), f32),
                pltpu.VMEM((2, zw, ny, nx), f32),
                pltpu.VMEM((STEPS, zw, ny, nx), f32),
                pltpu.VMEM((3, zw, ny, nx), f32),
                pltpu.VMEM((3 * nx, nx), jnp.bfloat16),
                pltpu.VMEM((32, nx), f32),
                pltpu.VMEM((group, 8, tw), f32),
            ]
            + [dma((nd,))] * 4
            + [dma((nd + 1,))] * 8
            + [dma((group,))] * 2
            + [pltpu.SMEM(a.shape, a.dtype) for a in (wavelet, sz, sy, sx, seeds, rz, ry, rx)]
            + [dma((11,))],
            compiler_params=pltpu.CompilerParams(
                collective_id=0, has_side_effects=True, vmem_limit_bytes=60 << 20
            ),
        )(wavelet, sz, sy, sx, seeds, rz, ry, rx, courant, prev, now)
        if not split:
            pw0 = width // lax.axis_size("rep")
            inc = lax.dynamic_slice_in_dim(inc, lax.axis_index("rep") * pw0, pw0, 2)
        return inc, wave, traces

    return jax.shard_map(
        shards,
        mesh=mesh,
        in_specs=(
            P("slab", "sub", None),
            P(("shot", "slab"), "sub", "rep"),
            P(("shot", "slab"), "sub", "rep"),
            P(),
            P("shot"),
            P("shot"),
            P("shot"),
            P("rep"),
            P(),
            P(),
            P(),
        ),
        out_specs=(
            P(("shot", "slab"), "sub", "rep"),
            P("rep", ("shot", "slab"), "sub", None),
            P("shot", "rep", None),
        ),
        check_vma=False,
    )
```
